32 devices in a mesh: segment: 2 (over x), rows: 8 (over z, y), cols: 2 (over core).
Axes of the slice: x: 2, y: 2, z: 4, core: 2. Of those that a mesh axis runs over, the one named last changes fastest.
Arguments:
- frames: bfloat16 [2, 2, 16, 128, 128], P(None, None, 'rows', 'cols'), may hold values from -6 to 6
- cell_weight: bfloat16 [9, 256, 512], P(None, 'rows'), may hold values from -0.125 to 0.125
- cell_bias: float32 [512], replicated, may hold values from -3 to 3
- first_context_weight: bfloat16 [9, 128, 384], P(None, 'rows'), may hold values from -1 to 1
- first_context_bias: float32 [384], replicated, may hold values from -0.5 to 1
- second_context_weight: bfloat16 [9, 384, 384], P(None, 'rows'), may hold values from -0.109375 to 0.109375
- second_context_bias: float32 [384], replicated, may hold values from -0.5 to 1
- third_context_weight: bfloat16 [9, 384, 384], P(None, 'rows'), may hold values from -0.109375 to 0.109375
- third_context_bias: float32 [384], replicated, may hold values from 0 to 1
Outputs:
- context: bfloat16 [2, 16, 128, 384], P('segment', 'rows', 'cols')
The draws below stay inside these ranges and needn't reach their ends.
All inputs are finite; a program needn't handle non-finite values.
Results may differ from the reference program's by a relative error of at most 0.0065.
Values may be sent and summed in bfloat16 or wider, within the bound.
A program may use at most 64 MiB of HBM per device.

```python
import jax
import jax.numpy as jnp
from jax import lax

C = 128
CIN = 128
K = 384
STEPS = 2
MB = 2
FIRST_DILATION = 16
SECOND_DILATION = 32
THIRD_DILATION = 64
NH = 16
NW = 128


def shard_levels(own_key, dims, shards, smallest, largest):
    level, own = 1.0, jax.random.fold_in(own_key, 6)
    for dim, parts in shards:
        heights = jnp.exp(jax.random.uniform(jax.random.fold_in(own, dim), (parts,), jnp.float32, smallest / len(shards), largest / len(shards)))
        level = level * jnp.repeat(heights, dims[dim] // parts).reshape([-1 if axis == dim else 1 for axis in range(len(dims))])
    return level


def centred(stream_key, shape, width, reach, pieces=(), dtype=jnp.bfloat16):
    level = shard_levels(stream_key, shape, pieces, -0.22, 0.18) if pieces else 1.0
    values = jax.random.normal(stream_key, shape, jnp.float32) * width * level
    return jnp.minimum(jnp.maximum(values, -reach), reach).astype(dtype)


def setup_inputs(seed: int = 0) -> dict:
    streams_of = jax.random.split(jax.random.key(seed), 10)
    frames = centred(streams_of[0], (MB, STEPS, NH, NW, CIN), 1.0, 6.0, ((2, 8), (3, 2)))
    cell_weight = centred(streams_of[1], (9, CIN + C, 4 * C), (9 * (CIN + C)) ** -0.5, 0.125, ((1, 8),))
    cell_bias = centred(streams_of[2], (4 * C,), 0.5, 3.0, (), jnp.float32)
    first_context_weight = centred(streams_of[3], (9, C, K), (C // 4) ** -0.5, 1.0, ((1, 8),))
    first_context_bias = jnp.clip(jax.random.uniform(streams_of[4], (K,), jnp.float32, -0.5, 1.0), -0.5, 1.0)
    second_context_weight = centred(streams_of[5], (9, K, K), (9 * K) ** -0.5, 0.109375, ((1, 8),))
    second_context_bias = jnp.clip(jax.random.uniform(streams_of[6], (K,), jnp.float32, -0.5, 1.0), -0.5, 1.0)
    third_context_weight = centred(streams_of[7], (9, K, K), (9 * K) ** -0.5, 0.109375, ((1, 8),))
    third_context_bias = jnp.clip(jax.random.uniform(streams_of[8], (K,), jnp.float32, 0.0, 1.0), 0.0, 1.0)
    return dict(frames=frames, cell_weight=cell_weight, cell_bias=cell_bias, first_context_weight=first_context_weight, first_context_bias=first_context_bias, second_context_weight=second_context_weight, second_context_bias=second_context_bias, third_context_weight=third_context_weight, third_context_bias=third_context_bias)


def dilated_convolve(feature, weight, spacing):
    kernel = weight.astype(jnp.float32).reshape(3, 3, weight.shape[1], weight.shape[2])
    result = lax.conv_general_dilated(
        feature.astype(jnp.float32)[None], kernel, (1, 1),
        [(spacing, spacing), (spacing, spacing)], rhs_dilation=(spacing, spacing),
        dimension_numbers=("NHWC", "HWIO", "NHWC"), precision=lax.Precision.HIGHEST)
    return result[0]


def reference(frames, cell_weight, cell_bias, first_context_weight, first_context_bias, second_context_weight, second_context_bias, third_context_weight, third_context_bias):
    outputs = []
    for micro_index in range(MB):
        hidden_state = jnp.zeros((NH, NW, C), jnp.bfloat16)
        memory = jnp.zeros((NH, NW, C), jnp.float32)
        for moment in range(STEPS):
            joined = jnp.concatenate([frames[micro_index, moment], hidden_state], axis=-1)
            gate_sums = dilated_convolve(joined, cell_weight, 1) + cell_bias
            inflow = jax.nn.sigmoid(gate_sums[..., :C])
            forget = jax.nn.sigmoid(gate_sums[..., C:2 * C])
            output = jax.nn.sigmoid(gate_sums[..., 2 * C:3 * C])
            update = jnp.tanh(gate_sums[..., 3 * C:])
            memory = forget * memory + inflow * update
            hidden_state = (output * jnp.tanh(memory)).astype(jnp.bfloat16)
        first_output = jnp.maximum(dilated_convolve(hidden_state, first_context_weight, FIRST_DILATION) + first_context_bias, 0.0).astype(jnp.bfloat16)
        second_output = jnp.maximum(dilated_convolve(first_output, second_context_weight, SECOND_DILATION) + second_context_bias, 0.0).astype(jnp.bfloat16)
        third_output = jnp.maximum(dilated_convolve(second_output, third_context_weight, THIRD_DILATION) + third_context_bias, 0.0)
        outputs.append((second_output.astype(jnp.float32) + third_output).astype(jnp.bfloat16))
    return jnp.stack(outputs)
```

```python
import functools

import jax
import jax.numpy as jnp
from jax import lax
from jax.experimental import pallas as pl
from jax.experimental.pallas import tpu as pltpu
from jax.sharding import PartitionSpec as P

DILATIONS = (16, 32, 64)
MESH_ID = pl.DeviceIdType.MESH
MARGIN = 16


def encoder_kernel(
    frames, cell_w, cell_b, first_w, first_b, second_w, second_b, third_w, third_b,
    out, wc, w1, w2, w3, fp, hp, f1, f2, f3,
    local_sem, ring_s, ring_r, across_s, across_r, pair_s, pair_r, ex_s, ex_r, *, n, cols, shared, row_pads,
):
    seg, r, c = lax.axis_index("segment"), lax.axis_index("rows"), lax.axis_index("cols")
    steps, height, across, channels = frames.shape[1:]
    state = cell_b.shape[-1] // 4
    half = n // 2
    odd = lax.rem(c, 2)
    even_core, odd_core = odd == 0, odd == 1
    sign = 1 - 2 * odd
    parity, pair = lax.rem(r, 2), lax.div(r, 2)
    place = pair + parity * (n - 1 - 2 * pair)

    def rows_at(position):
        upper = lax.div(position, half)
        return 2 * position + upper * (2 * n - 1 - 4 * position)

    behind_rows = [r] + [rows_at(lax.rem(place - sign * k + n, n)) for k in range(1, half + 1)]
    ahead_rows = [r] + [rows_at(lax.rem(place + sign * k + n, n)) for k in range(1, half + 1)]
    following, preceding = ahead_rows[1], behind_rows[1]
    partner = c + 1 - 2 * odd
    ahead_id, partner_id = (seg, following, c), (seg, r, partner)

    reaches = sorted({1} | {s // height for s, pad in zip(DILATIONS, row_pads) if pad})
    offsets = [(0, -1), (0, 1)] + [
        (d * reach, dc) for reach in reaches for d in (-1, 1) for dc in (-1, 0, 1)
    ]

    def present(dr, dc):
        row, col = r + dr, c + dc
        return jnp.logical_and(
            jnp.logical_and(row >= 0, row < n), jnp.logical_and(col >= 0, col < cols)
        )

    inside = {offset: present(*offset) for offset in offsets}

    locals_ = []
    for t in range(steps):
        locals_.append(
            pltpu.make_async_copy(
                frames.at[seg, t],
                fp.at[t, pl.ds(1, height), pl.ds(MARGIN, across)],
                local_sem.at[t],
            )
        )
    stored = (cell_w, first_w, second_w, third_w)
    gathered = (wc, w1, w2, w3)
    own = []
    for ref, whole in zip(stored, gathered):
        taps = whole.shape[1]
        own.append(ref.at[pl.ds((9 - taps) // 2, taps)])
    for a in range(4):
        locals_.append(
            pltpu.make_async_copy(own[a], gathered[a].at[r], local_sem.at[steps + a])
        )
    for t in range(steps):
        fp[t] = jnp.zeros(fp.shape[1:], fp.dtype)
    for t in range(hp.shape[0]):
        hp[t] = jnp.zeros(hp.shape[1:], hp.dtype)
    for buffer in (f1, f2, f3):
        buffer[...] = jnp.zeros(buffer.shape, buffer.dtype)
    for copy in locals_:
        copy.start()

    barrier = pltpu.get_barrier_semaphore()
    expected = jnp.int32(2)
    for target in (following, preceding):
        pl.semaphore_signal(barrier, inc=1, device_id=(seg, target, c), device_id_type=MESH_ID)
    for dr, dc in offsets:
        there = inside[dr, dc]
        expected = expected + there.astype(jnp.int32)

        @pl.when(there)
        def _():
            pl.semaphore_signal(
                barrier, inc=1, device_id=(seg, r + dr, c + dc), device_id_type=MESH_ID
            )

    if shared:
        expected = expected + 1
        pl.semaphore_signal(barrier, inc=1, device_id=(1 - seg, r, c), device_id_type=MESH_ID)
    pl.semaphore_wait(barrier, expected)

    def exchange(number, source_of, buffer, pad, reach, width):
        arrivals, departures = [], []
        for i, (dr, dc) in enumerate((a, b) for a in (-1, 0, 1) for b in (-1, 0, 1)):
            if (dr, dc) == (0, 0) or (dr and not pad):
                continue
            first, span, landing = {
                -1: (0, pad, pad + height), 0: (0, height, pad), 1: (height - pad, pad, 0)
            }[dr]
            left, extent, side = {
                -1: (0, width[1], width[0] + across),
                0: (0, across, width[0]),
                1: (across - width[1], width[1], width[0] - width[1]),
            }[dc]
            copy = pltpu.make_async_remote_copy(
                src_ref=source_of(first, span, left, extent),
                dst_ref=buffer.at[pl.ds(landing, span), pl.ds(side, extent)],
                send_sem=ex_s.at[number, i],
                recv_sem=ex_r.at[number, i],
                device_id=(seg, r + dr * reach, c + dc),
                device_id_type=MESH_ID,
            )
            there, behind = inside[dr * reach, dc], inside[-dr * reach, -dc]
            pl.when(there)(copy.start)
            departures.append((there, copy))
            arrivals.append((behind, copy))

        def arrive():
            for behind, copy in arrivals:
                pl.when(behind)(copy.wait_recv)

        def depart():
            for there, copy in departures:
                pl.when(there)(copy.wait_send)

        return arrive, depart

    def block_of(buffer, pad, margin):
        return lambda first, span, left, extent: buffer.at[
            pl.ds(pad + first, span), pl.ds(margin + left, extent)
        ]

    departs = []
    frame_arrivals = []
    for t in range(steps):
        arrive, depart = exchange(
            t,
            lambda first, span, left, extent, t=t: frames.at[
                seg, t, pl.ds(first, span), pl.ds(left, extent)
            ],
            fp.at[t], 1, 1, (MARGIN, MARGIN),
        )
        frame_arrivals.append(arrive)
        departs.append(depart)

    parts = (2 * seg, 1, 2 * (1 - seg)) if shared else (0, 1, 2)
    carried = range(2) if shared else range(3)

    def slot(a, part, k):
        span = gathered[a].shape[1] // 3
        source = behind_rows[k] if k >= 0 else ahead_rows[-k]
        return gathered[a].at[source, pl.ds(parts[part] * span, span)]

    def ring_copy(a, part, k, sent=True):
        span = gathered[a].shape[1] // 3
        place_of = slot(a, part, k if sent else k + 1)
        start = (9 - 3 * span) // 2 + parts[part] * span
        return pltpu.make_async_remote_copy(
            src_ref=stored[a].at[pl.ds(start, span)] if sent and k == 0 else place_of,
            dst_ref=place_of,
            send_sem=ring_s.at[a, part, k],
            recv_sem=ring_r.at[a, part, k],
            device_id=ahead_id,
            device_id_type=MESH_ID,
        )

    def across_copy(a, k, sent=True):
        piece = slot(a, 0 if sent else 2, k)
        return pltpu.make_async_remote_copy(
            src_ref=piece, dst_ref=piece, send_sem=across_s.at[a, k], recv_sem=across_r.at[a, k],
            device_id=(1 - seg, r, c), device_id_type=MESH_ID,
        )

    def pair_copy(a, part, k, direction):
        piece = slot(a, part, direction * k)
        return pltpu.make_async_remote_copy(
            src_ref=piece, dst_ref=piece, send_sem=pair_s.at[a, part, k],
            recv_sem=pair_r.at[a, part, k], device_id=partner_id, device_id_type=MESH_ID,
        )

    def longer(a):
        return even_core if a == 0 else odd_core

    def guarded(condition, act):
        if condition is None:
            act()
        else:
            pl.when(condition)(act)

    def ring_send(a, part, k):
        guarded(longer(a) if k == half - 1 else None, ring_copy(a, part, k).start)

    def own_send(a):
        for part in carried:
            ring_send(a, part, 0)

    def ring_step(a, k):
        def act():
            for part in carried:
                ring_copy(a, part, k - 1, False).wait_recv()
                if k < half:
                    ring_send(a, part, k)
                if shared and part == 0:
                    across_copy(a, k).start()
                pair_copy(a, part, k, 1).start()

        guarded(longer(a) if k == half else None, act)

    def across_step(a, k):
        def act():
            across_copy(a, k, False).wait_recv()
            pair_copy(a, 2, k, 1).start()

        if shared:
            guarded(longer(a) if k == half else None, act)

    def pair_waits(a):
        shorter = odd_core if a == 0 else even_core
        for k in range(1, half + 1):
            for part in range(3):
                guarded(
                    shorter if k == half else None, pair_copy(a, part, k, -1).wait_recv
                )

    context_steps = list(range(1, half + 1))
    quarter = max(1, half // 4)

    def context_ring(count):
        for _ in range(min(count, len(context_steps))):
            k = context_steps.pop(0)
            for a in (1, 2, 3):
                ring_step(a, k)
            if k > 1:
                for a in (1, 2, 3):
                    across_step(a, k - 1)

    own_send(0)
    for k in range(1, half + 1):
        ring_step(0, k)
        if k > 1:
            across_step(0, k - 1)
        if k == 1:
            for a in (1, 2, 3):
                own_send(a)
        else:
            context_ring(1)
    context_ring(quarter)
    across_step(0, half)

    for copy in locals_:
        copy.wait()
    for arrive in frame_arrivals:
        arrive()
    pair_waits(0)

    bias = cell_b[...].reshape(1, -1)
    per = wc.shape[2]
    frame_sources = channels // per

    def tap_columns(buffer):
        taps = []
        for row in range(height + 2):
            wide = buffer[row].astype(jnp.float32)
            length = wide.shape[0]
            taps.append(
                [
                    pltpu.roll(wide, 1, 0)[MARGIN : MARGIN + across].astype(jnp.bfloat16),
                    buffer[row, MARGIN : MARGIN + across],
                    pltpu.roll(wide, length - 1, 0)[MARGIN : MARGIN + across].astype(
                        jnp.bfloat16
                    ),
                ]
            )
        return taps

    def gate_part(buffer, sources):
        taps = tap_columns(buffer)
        left = jnp.concatenate(
            [
                jnp.concatenate([taps[row + a][b] for row in range(height)], axis=0)
                for a in range(3)
                for b in range(3)
            ],
            axis=1,
        )
        right = jnp.concatenate([wc[s, t] for t in range(9) for s in sources], axis=0)
        return jnp.dot(left, right, preferred_element_type=jnp.float32)

    def update(gates, memory):
        inflow = jax.nn.sigmoid(gates[:, :state])
        forget = jax.nn.sigmoid(gates[:, state : 2 * state])
        output = jax.nn.sigmoid(gates[:, 2 * state : 3 * state])
        fresh = inflow * jnp.tanh(gates[:, 3 * state :])
        memory = fresh if memory is None else forget * memory + fresh
        return (output * jnp.tanh(memory)).astype(jnp.bfloat16), memory

    seen, unseen = range(frame_sources), range(frame_sources, n)
    hidden, memory = update(gate_part(fp.at[0], seen) + bias, None)
    for t in range(1, steps):
        view = hp.at[t - 1]
        for row in range(height):
            view[1 + row, MARGIN : MARGIN + across] = hidden[row * across : (row + 1) * across]
        arrive, depart = exchange(
            steps + t - 1, block_of(view, 1, MARGIN), view, 1, 1, (MARGIN, MARGIN)
        )
        departs.append(depart)
        context_ring(quarter)
        gates = gate_part(fp.at[t], seen) + bias
        context_ring(quarter)
        arrive()
        hidden, memory = update(gates + gate_part(view, unseen), memory)

    feature = hidden
    layers = ((f1, w1, first_b), (f2, w2, second_b), (f3, w3, third_b))
    for i, (buffer, weight, offset) in enumerate(layers):
        spacing, pad = DILATIONS[i], row_pads[i]
        for row in range(height):
            buffer[pad + row, spacing : spacing + across] = feature[
                row * across : (row + 1) * across
            ]
        arrive, depart = exchange(
            2 * steps - 1 + i, block_of(buffer, pad, spacing), buffer, pad,
            spacing // height, (spacing, spacing),
        )
        departs.append(depart)
        if i == 0:
            context_ring(len(context_steps))
            for a in (1, 2, 3):
                across_step(a, half)
        pair_waits(i + 1)
        arrive()
        total = None
        taps = weight.shape[1]
        for t in range(taps):
            a, b = t // 3, t % 3
            left = buffer[a * pad : a * pad + height, b * spacing : b * spacing + across]
            left = left.reshape(height * across, left.shape[-1])
            right = jnp.concatenate([weight[s, t] for s in range(n)], axis=0)
            product = jnp.dot(left, right, preferred_element_type=jnp.float32)
            total = product if total is None else total + product
        result = jnp.maximum(total + offset[...].reshape(1, -1), 0.0)
        if i < 2:
            feature = result.astype(jnp.bfloat16)
    context = (feature.astype(jnp.float32) + result).astype(jnp.bfloat16)
    out[0] = context.reshape(out.shape[1:])

    for depart in departs:
        depart()
    for a in range(4):
        for k in range(half):
            for part in carried:
                guarded(
                    longer(a) if k == half - 1 else None, ring_copy(a, part, k).wait_send
                )
        for k in range(1, half + 1):
            for part in range(3):
                guarded(longer(a) if k == half else None, pair_copy(a, part, k, 1).wait_send)
            if shared:
                guarded(longer(a) if k == half else None, across_copy(a, k).wait_send)


def per_device(n, cols, shared, *args):
    frames, cell_w, cell_b, first_w, first_b, second_w, second_b, third_w, third_b = args
    micro, steps, height, across, channels = frames.shape
    state, width = cell_b.shape[0] // 4, first_b.shape[0]
    row_pads = tuple(height if s // height < n else 0 for s in DILATIONS)

    def slots(weight, pad):
        return pltpu.VMEM((n, 9 if pad else 3) + weight.shape[1:], weight.dtype)

    def field(spacing, pad, depth):
        return pltpu.VMEM((height + 2 * pad, across + 2 * spacing, depth), jnp.bfloat16)

    half = n // 2
    exchanges = 2 * steps - 1 + 3
    dma = pltpu.SemaphoreType.DMA
    anywhere, vmem = pl.BlockSpec(memory_space=pl.ANY), pl.BlockSpec(memory_space=pltpu.VMEM)
    return pl.pallas_call(
        functools.partial(encoder_kernel, n=n, cols=cols, shared=shared, row_pads=row_pads),
        out_shape=jax.ShapeDtypeStruct((1, height, across, width), jnp.bfloat16),
        in_specs=[anywhere, anywhere, vmem, anywhere, vmem, anywhere, vmem, anywhere, vmem],
        out_specs=vmem,
        scratch_shapes=[
            slots(cell_w, 1),
            slots(first_w, row_pads[0]),
            slots(second_w, row_pads[1]),
            slots(third_w, row_pads[2]),
            pltpu.VMEM((steps, height + 2, across + 2 * MARGIN, channels), jnp.bfloat16),
            pltpu.VMEM((steps - 1, height + 2, across + 2 * MARGIN, state), jnp.bfloat16),
            field(DILATIONS[0], row_pads[0], state),
            field(DILATIONS[1], row_pads[1], width),
            field(DILATIONS[2], row_pads[2], width),
            dma((steps + 4,)),
            dma((4, 3, half)),
            dma((4, 3, half)),
            dma((4, half + 1)),
            dma((4, half + 1)),
            dma((4, 3, half + 1)),
            dma((4, 3, half + 1)),
            dma((exchanges, 9)),
            dma((exchanges, 9)),
        ],
        compiler_params=pltpu.CompilerParams(collective_id=0, has_side_effects=True),
    )(
        frames, cell_w, cell_b, first_w, first_b, second_w, second_b,
        third_w, third_b,
    )


def grid_kernel(
    frames, cell_w, cell_b, first_w, first_b, second_w, second_b, third_w, third_b,
    out, wc, w1, w23, fp, hp, f1, f2, f3,
    local_sem, link_s, link_r, own_s, own_r, twin_s, twin_r, twin_own_s, twin_own_r,
    ex_s, ex_r, col_s, col_r, *, n,
):
    x, r, c = lax.axis_index("segment"), lax.axis_index("rows"), lax.axis_index("cols")
    steps, height, across, channels = frames.shape[1:]
    state = cell_b.shape[-1] // 4
    planes = n // 2
    reach = planes - 1
    z, y = lax.div(r, 2), lax.rem(r, 2)
    ry = r + 1 - 2 * y
    twin = 1 - c
    even_core, odd_core = c == 0, c == 1
    wide = lax.rem(x + c, 2) == 0
    narrow = jnp.logical_not(wide)
    ways = (-1, 1)

    def run(conditions, act):
        known = [condition for condition in conditions if condition is not None]
        if not known:
            act()
            return
        total = known[0]
        for condition in known[1:]:
            total = jnp.logical_and(total, condition)
        pl.when(total)(act)

    pads = [steps - t for t in range(steps)]
    locals_ = [
        pltpu.make_async_copy(
            cell_w.at[:, :, pl.ds(half * 2 * state, 2 * state)], wc.at[half, r],
            local_sem.at[half],
        )
        for half in range(2)
    ]
    locals_.append(pltpu.make_async_copy(first_w.at[pl.ds(3, 3)], w1.at[r], local_sem.at[2]))
    locals_.append(
        pltpu.make_async_copy(second_w.at[pl.ds(3, 3)], w23.at[0, r], local_sem.at[3])
    )
    locals_.append(
        pltpu.make_async_copy(third_w.at[pl.ds(3, 3)], w23.at[1, r], local_sem.at[4])
    )
    for t in range(steps):
        locals_.append(
            pltpu.make_async_copy(
                frames.at[x, t],
                fp.at[t, pl.ds(pads[t], height), pl.ds(MARGIN, across)],
                local_sem.at[5 + t],
            )
        )
    for copy in locals_:
        copy.start()

    def row_inside(row):
        return jnp.logical_and(row >= 0, row < n)

    def plane_inside(plane):
        return jnp.logical_and(plane >= 0, plane < planes)

    barrier = pltpu.get_barrier_semaphore()
    expected = jnp.int32(2)
    pl.semaphore_signal(barrier, inc=1, device_id=(1 - x, r, c), device_id_type=MESH_ID)
    pl.semaphore_signal(barrier, inc=1, device_id=(x, r, twin), device_id_type=MESH_ID)
    for d in ways:
        for core in (c, twin):
            there = row_inside(r + d)
            expected = expected + there.astype(jnp.int32)

            @pl.when(there)
            def _():
                pl.semaphore_signal(
                    barrier, inc=1, device_id=(x, r + d, core), device_id_type=MESH_ID
                )

        for k in range(1, reach + 1):
            there = plane_inside(z + d * k)
            expected = expected + there.astype(jnp.int32)

            @pl.when(there)
            def _():
                pl.semaphore_signal(
                    barrier, inc=1, device_id=(x, r + 2 * d * k, c), device_id_type=MESH_ID
                )

    pl.semaphore_wait(barrier, expected)

    kinds = 3
    holder = (None, odd_core, None)
    taker = (None, even_core, None)
    per_third = (3, 1, 1)

    def piece(a, half, s, third, count):
        taps = pl.ds(third * per_third[a], count * per_third[a])
        if a == 0:
            return wc.at[half, s, taps]
        if a == 1:
            return w1.at[s, taps]
        return w23.at[half, s, taps]

    def slot(k, d):
        return 2 * (k - 1) + (d + 1) // 2

    def link(kind, a, k, d, ref, device):
        return pltpu.make_async_remote_copy(
            src_ref=ref, dst_ref=ref, send_sem=link_s.at[a, kind, slot(k, d)],
            recv_sem=link_r.at[a, kind, slot(k, d)], device_id=device, device_id_type=MESH_ID,
        )

    def both(kind, a, k, d, ref):
        return pltpu.make_async_remote_copy(
            src_ref=ref, dst_ref=ref, send_sem=twin_s.at[a, kind, slot(k, d)],
            recv_sem=twin_r.at[a, kind, slot(k, d)], device_id=(x, r, twin),
            device_id_type=MESH_ID,
        )

    def shapes(first, one, two):
        return ((first, *two), (jnp.logical_not(first), *one))

    lower, mine, other = x, 2 * x, 2 * (1 - x)
    z_span = ((None, lower, 2),)
    x_span = ((None, other, 1),)
    x_sent = ((None, mine, 1),)
    y_span = shapes(wide, (mine, 1), (lower, 2))
    r_span = shapes(narrow, (other, 1), (1 - x, 2))
    y_twin = shapes(narrow, (mine, 1), (lower, 2))
    r_twin = shapes(wide, (other, 1), (1 - x, 2))
    departures = []

    def send(kind, a, k, d, s, spans, there, device, make=link):
        for condition, third, count in spans:
            def act(third=third, count=count, wait=False):
                copy = make(kind, a, k, d, piece(a, c, s, third, count), device)
                (copy.wait_send if wait else copy.start)()

            run([holder[a], there, condition], act)
            departures.append(
                ([holder[a], there, condition], functools.partial(act, wait=True))
            )

    def chained(a, k):
        return a > 0 and k > 2

    def z_send(a, k, d):
        if chained(a, k):
            there = jnp.logical_and(plane_inside(z + d), plane_inside(z - d * (k - 1)))
            send(0, a, k, d, r - 2 * d * (k - 1), z_span, there, (x, r + 2 * d, c))
        else:
            send(0, a, k, d, r, z_span, plane_inside(z + d * k), (x, r + 2 * d * k, c))

    def twin_make(kind, a, k, d, ref, device):
        return both(kind, a, k, d, ref)

    def receive(kind, a, k, d, s, spans, there):
        for condition, third, count in spans:
            def act(third=third, count=count):
                link(kind, a, k, d, piece(a, c, s, third, count), (x, r, twin)).wait_recv()

            run([holder[a], there, condition], act)

    def z_step(a, k):
        for d in ways:
            there, s = plane_inside(z - d * k), r - 2 * d * k
            receive(0, a, k, d, s, z_span, there)
            if k < reach and chained(a, k + 1):
                z_send(a, k + 1, d)
            send(2, a, k, d, s, y_span, there, (x, ry, c))
            send(1, a, k, d, s, x_sent, there, (1 - x, r, c))
            send(0, a, k, d, s, z_span, there, None, twin_make)

    def x_step(a, k):
        for d in ways:
            there, s = plane_inside(z - d * k), r - 2 * d * k
            receive(1, a, k, d, s, x_span, there)
            send(1, a, k, d, s, x_span, there, None, twin_make)

    def y_step(a, k):
        for d in ways:
            there, s = plane_inside(z - d * k), ry - 2 * d * k
            receive(2, a, k, d, s, y_span, there)
            send(3, a, k, d, s, y_span, there, (1 - x, r, c))
            send(2, a, k, d, s, y_span, there, None, twin_make)

    def relay_step(a, k):
        for d in ways:
            there, s = plane_inside(z - d * k), ry - 2 * d * k
            receive(3, a, k, d, s, r_span, there)
            send(3, a, k, d, s, r_span, there, None, twin_make)

    def own_copy(a, s):
        ref = piece(a, c, s, 0, 3)
        return pltpu.make_async_remote_copy(
            src_ref=ref, dst_ref=ref, send_sem=own_s.at[a], recv_sem=own_r.at[a],
            device_id=(x, ry, c), device_id_type=MESH_ID,
        )

    def own_twin(a, half):
        ref = piece(a, half, ry, 0, 3)
        return pltpu.make_async_remote_copy(
            src_ref=ref, dst_ref=ref, send_sem=twin_own_s.at[a], recv_sem=twin_own_r.at[a],
            device_id=(x, r, twin), device_id_type=MESH_ID,
        )

    def own_send(a):
        run([holder[a]], lambda: own_copy(a, r).start())
        departures.append(([holder[a]], lambda: own_copy(a, r).wait_send()))

    def own_step(a, _):
        def act():
            own_copy(a, ry).wait_recv()
            own_twin(a, c).start()

        run([holder[a]], act)
        departures.append(([holder[a]], lambda: own_twin(a, c).wait_send()))

    def twin_waits(a):
        run([taker[a]], lambda: own_twin(a, twin).wait_recv())
        for k in range(1, reach + 1):
            for d in ways:
                there = plane_inside(z - d * k)
                for kind, spans, base in (
                    (0, z_span, r), (1, x_span, r), (2, y_twin, ry), (3, r_twin, ry)
                ):
                    for condition, third, count in spans:
                        ref_of = functools.partial(
                            piece, a, twin, base - 2 * d * k, third, count
                        )
                        run(
                            [taker[a], there, condition],
                            lambda kind=kind, ref_of=ref_of: both(
                                kind, a, k, d, ref_of()
                            ).wait_recv(),
                        )

    for copy in locals_[:2]:
        copy.wait()
    for k in range(1, reach + 1):
        for d in ways:
            z_send(0, k, d)
    own_send(0)

    offsets = [(dr, dc) for dr in (-1, 0, 1) for dc in (-1, 0, 1) if (dr, dc) != (0, 0)]

    def inside(dr, dc):
        col = c + dc
        return jnp.logical_and(row_inside(r + dr), jnp.logical_and(col >= 0, col < 2))

    frame_arrivals = []
    for t in range(steps):
        pad = pads[t]
        for i, (dr, dc) in enumerate(offsets):
            first, span, landing = {
                -1: (0, pad, pad + height), 0: (0, height, pad), 1: (height - pad, pad, 0)
            }[dr]
            left, extent, side = {
                -1: (0, MARGIN, MARGIN + across),
                0: (0, across, MARGIN),
                1: (across - MARGIN, MARGIN, 0),
            }[dc]
            copy = pltpu.make_async_remote_copy(
                src_ref=frames.at[x, t, pl.ds(first, span), pl.ds(left, extent)],
                dst_ref=fp.at[t, pl.ds(landing, span), pl.ds(side, extent)],
                send_sem=ex_s.at[t, i],
                recv_sem=ex_r.at[t, i],
                device_id=(x, r + dr, c + dc),
                device_id_type=MESH_ID,
            )
            run([inside(dr, dc)], copy.start)
            departures.append(([inside(dr, dc)], copy.wait_send))
            frame_arrivals.append(([inside(-dr, -dc)], copy.wait_recv))

    for copy in locals_[2:5]:
        copy.wait()
    for a in range(1, kinds):
        for k in range(1, reach + 1):
            for d in ways:
                if not chained(a, k):
                    z_send(a, k, d)
        own_send(a)

    depth = fp.shape[-1]
    for t in range(steps):
        pad = pads[t]
        total_rows = height + 2 * pad

        def blank(ref, first, count, left, extent):
            ref[first : first + count, left : left + extent] = jnp.zeros(
                (count, extent, ref.shape[-1]), ref.dtype
            )

        @pl.when(r == 0)
        def _(t=t, pad=pad):
            blank(fp.at[t], 0, pad, 0, across + 2 * MARGIN)

        @pl.when(r == n - 1)
        def _(t=t, pad=pad):
            blank(fp.at[t], pad + height, pad, 0, across + 2 * MARGIN)

        @pl.when(even_core)
        def _(t=t, total_rows=total_rows):
            blank(fp.at[t], 0, total_rows, 0, MARGIN)

        @pl.when(odd_core)
        def _(t=t, total_rows=total_rows):
            blank(fp.at[t], 0, total_rows, MARGIN + across, MARGIN)

    fields = [(hp.at[t], MARGIN) for t in range(steps - 1)]
    fields += [(f1, DILATIONS[0]), (f2, DILATIONS[1])]
    for ref, margin in fields:
        @pl.when(even_core)
        def _(ref=ref, margin=margin):
            blank(ref, 0, ref.shape[0], 0, margin)

        @pl.when(odd_core)
        def _(ref=ref, margin=margin):
            blank(ref, 0, ref.shape[0], margin + across, margin)

    plan = []
    for a, start, pace in ((0, 2.2, 2.1), (1, 9.5, 1.0), (2, 10.0, 2.0)):
        plan.append((start + 3.2, own_step, a, 0))
        for k in range(1, reach + 1):
            there = start + pace * k
            plan.append((there, z_step, a, k))
            plan.append((there + 3.0, x_step, a, k))
            plan.append((there + 3.5, y_step, a, k))
            plan.append((there + 7.0, relay_step, a, k))
    plan.sort(key=lambda entry: entry[0])

    def advance(last):
        while plan and (last is None or plan[0][0] <= last):
            _, step, a, k = plan.pop(0)
            step(a, k)

    advance(2.2 + 2.1 * reach + 7.0)

    for copy in locals_[5:]:
        copy.wait()
    for conditions, act in frame_arrivals:
        run(conditions, act)
    twin_waits(0)

    bias = cell_b[...].reshape(1, -1)
    per = wc.shape[3]
    frame_sources = channels // per

    def tap_columns(buffer, count):
        taps = []
        for row in range(count):
            wide_row = buffer[row].astype(jnp.float32)
            length = wide_row.shape[0]
            taps.append(
                [
                    pltpu.roll(wide_row, 1, 0)[MARGIN : MARGIN + across].astype(jnp.bfloat16),
                    buffer[row, MARGIN : MARGIN + across],
                    pltpu.roll(wide_row, length - 1, 0)[MARGIN : MARGIN + across].astype(
                        jnp.bfloat16
                    ),
                ]
            )
        return taps

    def columns_of(buffer, count):
        taps = tap_columns(buffer, count + 2)
        return jnp.concatenate(
            [
                jnp.concatenate([taps[row + a][b] for row in range(count)], axis=0)
                for a in range(3)
                for b in range(3)
            ],
            axis=1,
        )

    def gate_part(left, sources):
        return [
            jnp.dot(
                left,
                jnp.concatenate([wc[half, s, t] for t in range(9) for s in sources], axis=0),
                preferred_element_type=jnp.float32,
            )
            for half in range(2)
        ]

    def update(gates, memory):
        inflow = jax.nn.sigmoid(gates[0][:, :state])
        output = jax.nn.sigmoid(gates[1][:, :state])
        fresh = inflow * jnp.tanh(gates[1][:, state:])
        if memory is None:
            memory = fresh
        else:
            memory = jax.nn.sigmoid(gates[0][:, state:]) * memory + fresh
        return (output * jnp.tanh(memory)).astype(jnp.bfloat16), memory

    swaps = []

    def exchange_columns(number, buffer, margin):
        sent = pl.multiple_of((1 - c) * across + c * margin, 16)
        landing = pl.multiple_of(c * (margin + across), 16)
        copy = pltpu.make_async_remote_copy(
            src_ref=buffer.at[:, pl.ds(sent, margin)],
            dst_ref=buffer.at[:, pl.ds(landing, margin)],
            send_sem=col_s.at[number],
            recv_sem=col_r.at[number],
            device_id=(x, r, twin),
            device_id_type=MESH_ID,
        )
        copy.start()
        departures.append(([], copy.wait_send))
        return copy

    seen, unseen = range(frame_sources), range(frame_sources, n)
    counts = [height + 2 * (steps - 1 - t) for t in range(steps)]
    lefts = jnp.concatenate(
        [columns_of(fp.at[t], counts[t]) for t in range(steps)], axis=0
    )
    frame_gates = gate_part(lefts, seen)
    start = 0
    memory = None
    for t in range(steps):
        length = counts[t] * across
        gates = [
            part[start : start + length] + bias[:, half * 2 * state : (half + 1) * 2 * state]
            for half, part in enumerate(frame_gates)
        ]
        start += length
        if t:
            swaps[-1].wait_recv()
            extra = gate_part(columns_of(hp.at[t - 1], counts[t]), unseen)
            gates = [one + more for one, more in zip(gates, extra)]
            memory = memory[across : memory.shape[0] - across]
        hidden, memory = update(gates, memory)
        if t == steps - 1:
            break
        view = hp.at[t]
        outside = steps - 1 - t
        for row in range(counts[t]):
            value = hidden[row * across : (row + 1) * across]
            if row < outside or row >= counts[t] - outside:
                place = r * height + row - outside
                valid = jnp.logical_and(place >= 0, place < n * height)
                value = jnp.where(valid, value, jnp.zeros_like(value))
            view[row, MARGIN : MARGIN + across] = value
        swaps.append(exchange_columns(t, view, MARGIN))


    def product(left, weight):
        return jnp.dot(
            left.reshape(height * across, left.shape[-1]), weight,
            preferred_element_type=jnp.float32,
        )

    feature = hidden
    for i, (buffer, offset) in enumerate(((f1, first_b), (f2, second_b))):
        margin = DILATIONS[i]
        for row in range(height):
            buffer[row, margin : margin + across] = feature[row * across : (row + 1) * across]
        swap = exchange_columns(steps - 1 + i, buffer, margin)
        if i == 0:
            advance(9.5 + 1.0 * reach + 7.0)
            twin_waits(1)
        else:
            advance(None)
            twin_waits(2)

        def tap(b, i=i):
            store = w1 if i == 0 else w23.at[0]
            return jnp.concatenate([store[s, b] for s in range(n)], axis=0)

        total = product(feature, tap(1))
        swap.wait_recv()
        for b in (0, 2):
            total = total + product(buffer[:, b * margin : b * margin + across], tap(b))
        feature = jnp.maximum(total + offset[...].reshape(1, -1), 0.0).astype(jnp.bfloat16)
    f3[c] = feature.reshape(f3.shape[1:])
    swap = pltpu.make_async_remote_copy(
        src_ref=f3.at[c], dst_ref=f3.at[c], send_sem=col_s.at[steps + 1],
        recv_sem=col_r.at[steps + 1], device_id=(x, r, twin), device_id_type=MESH_ID,
    )
    swap.start()
    departures.append(([], swap.wait_send))

    def last(b):
        return jnp.concatenate([w23[1, s, b] for s in range(n)], axis=0)

    total = product(feature, last(1))
    pltpu.make_async_remote_copy(
        src_ref=f3.at[twin], dst_ref=f3.at[twin], send_sem=col_s.at[steps + 1],
        recv_sem=col_r.at[steps + 1], device_id=(x, r, twin), device_id_type=MESH_ID,
    ).wait_recv()
    total = total + product(f3[twin], last(2 - 2 * c))
    result = jnp.maximum(total + third_b[...].reshape(1, -1), 0.0)
    context = (feature.astype(jnp.float32) + result).astype(jnp.bfloat16)
    out[0] = context.reshape(out.shape[1:])

    for conditions, act in departures:
        run(conditions, act)


def grid_device(n, *args):
    frames, cell_w, cell_b, first_w, first_b, second_w, second_b, third_w, third_b = args
    micro, steps, height, across, channels = frames.shape
    state, width = cell_b.shape[0] // 4, first_b.shape[0]
    slots = 2 * (n // 2 - 1)
    dma, bf16 = pltpu.SemaphoreType.DMA, jnp.bfloat16
    anywhere, vmem = pl.BlockSpec(memory_space=pl.ANY), pl.BlockSpec(memory_space=pltpu.VMEM)
    return pl.pallas_call(
        functools.partial(grid_kernel, n=n),
        out_shape=jax.ShapeDtypeStruct((1, height, across, width), bf16),
        in_specs=[anywhere, anywhere, vmem, anywhere, vmem, anywhere, vmem, anywhere, vmem],
        out_specs=vmem,
        scratch_shapes=[
            pltpu.VMEM((2, n, 9, cell_w.shape[1], 2 * state), bf16),
            pltpu.VMEM((n, 3) + first_w.shape[1:], bf16),
            pltpu.VMEM((2, n, 3) + second_w.shape[1:], bf16),
            pltpu.VMEM((steps, height + 2 * steps, across + 2 * MARGIN, channels), bf16),
            pltpu.VMEM((steps - 1, height + 2 * (steps - 1), across + 2 * MARGIN, state), bf16),
            pltpu.VMEM((height, across + 2 * DILATIONS[0], state), bf16),
            pltpu.VMEM((height, across + 2 * DILATIONS[1], width), bf16),
            pltpu.VMEM((2, height, across, width), bf16),
            dma((5 + steps,)),
            dma((3, 4, slots)),
            dma((3, 4, slots)),
            dma((3,)),
            dma((3,)),
            dma((3, 4, slots)),
            dma((3, 4, slots)),
            dma((3,)),
            dma((3,)),
            dma((steps, 8)),
            dma((steps, 8)),
            dma((steps + 2,)),
            dma((steps + 2,)),
        ],
        compiler_params=pltpu.CompilerParams(collective_id=1, has_side_effects=True),
    )(*args)


def fits_grid(mesh, frames):
    n, cols = mesh.shape["rows"], mesh.shape["cols"]
    micro, steps, height, across, channels = frames.shape
    return (
        mesh.shape["segment"] == 2 and cols == 2 and n % 2 == 0 and n > 2
        and min(DILATIONS) // height >= n and DILATIONS[-1] == across
        and max(DILATIONS[:-1]) <= across and steps <= height
    )


def solution(mesh):
    kernels = P(None, "rows", None)
    placed = (
        P(None, None, "rows", "cols", None),
        kernels, P(), kernels, P(), kernels, P(), kernels, P(),
    )
    n, cols = mesh.shape["rows"], mesh.shape["cols"]

    def on_device(*args):
        if fits_grid(mesh, args[0]):
            return grid_device(n, *args)
        return per_device(n, cols, mesh.shape["segment"] == 2, *args)

    return jax.shard_map(
        on_device,
        mesh=mesh,
        in_specs=placed,
        out_specs=P("segment", "rows", "cols", None),
        check_vma=False,
    )
```

```python
import functools

import jax
import jax.numpy as jnp
from jax import lax
from jax.experimental import pallas as pl
from jax.experimental.pallas import tpu as pltpu
from jax.sharding import PartitionSpec as P

DILATIONS = (16, 32, 64)
MESH_ID = pl.DeviceIdType.MESH
MARGIN = 16
SENDS = 4.0
TIMES = ((3.2, 1.5, 3.2), (5.5, 2.0, 3.2), (9.0, 1.4, 3.2), (9.5, 1.5, 3.2))


def encoder_kernel(
    frames, cell_w, cell_b, first_w, first_b, second_w, second_b, third_w, third_b,
    out, wc, w1, w2, w3, fp, hp, f1, f2, f3,
    local_sem, ring_s, ring_r, across_s, across_r, pair_s, pair_r, ex_s, ex_r, *, n, cols, shared, row_pads,
):
    seg, r, c = lax.axis_index("segment"), lax.axis_index("rows"), lax.axis_index("cols")
    steps, height, across, channels = frames.shape[1:]
    state = cell_b.shape[-1] // 4
    half = n // 2
    odd = lax.rem(c, 2)
    even_core, odd_core = odd == 0, odd == 1
    sign = 1 - 2 * odd
    parity, pair = lax.rem(r, 2), lax.div(r, 2)
    place = pair + parity * (n - 1 - 2 * pair)

    def rows_at(position):
        upper = lax.div(position, half)
        return 2 * position + upper * (2 * n - 1 - 4 * position)

    behind_rows = [r] + [rows_at(lax.rem(place - sign * k + n, n)) for k in range(1, half + 1)]
    ahead_rows = [r] + [rows_at(lax.rem(place + sign * k + n, n)) for k in range(1, half + 1)]
    following, preceding = ahead_rows[1], behind_rows[1]
    partner = c + 1 - 2 * odd
    ahead_id, partner_id = (seg, following, c), (seg, r, partner)

    reaches = sorted({1} | {s // height for s, pad in zip(DILATIONS, row_pads) if pad})
    offsets = [(0, -1), (0, 1)] + [
        (d * reach, dc) for reach in reaches for d in (-1, 1) for dc in (-1, 0, 1)
    ]

    def present(dr, dc):
        row, col = r + dr, c + dc
        return jnp.logical_and(
            jnp.logical_and(row >= 0, row < n), jnp.logical_and(col >= 0, col < cols)
        )

    inside = {offset: present(*offset) for offset in offsets}

    locals_ = []
    for t in range(steps):
        locals_.append(
            pltpu.make_async_copy(
                frames.at[seg, t],
                fp.at[t, pl.ds(1, height), pl.ds(MARGIN, across)],
                local_sem.at[t],
            )
        )
    stored = (cell_w, first_w, second_w, third_w)
    gathered = (wc, w1, w2, w3)
    own = []
    for ref, whole in zip(stored, gathered):
        taps = whole.shape[1]
        own.append(ref.at[pl.ds((9 - taps) // 2, taps)])
    for a in range(4):
        locals_.append(
            pltpu.make_async_copy(own[a], gathered[a].at[r], local_sem.at[steps + a])
        )
    for t in range(steps):
        fp[t] = jnp.zeros(fp.shape[1:], fp.dtype)
    for t in range(hp.shape[0]):
        hp[t] = jnp.zeros(hp.shape[1:], hp.dtype)
    for buffer in (f1, f2, f3):
        buffer[...] = jnp.zeros(buffer.shape, buffer.dtype)
    for copy in locals_:
        copy.start()

    barrier = pltpu.get_barrier_semaphore()
    expected = jnp.int32(2)
    for target in (following, preceding):
        pl.semaphore_signal(barrier, inc=1, device_id=(seg, target, c), device_id_type=MESH_ID)
    for dr, dc in offsets:
        there = inside[dr, dc]
        expected = expected + there.astype(jnp.int32)

        @pl.when(there)
        def _():
            pl.semaphore_signal(
                barrier, inc=1, device_id=(seg, r + dr, c + dc), device_id_type=MESH_ID
            )

    if shared:
        expected = expected + 1
        pl.semaphore_signal(barrier, inc=1, device_id=(1 - seg, r, c), device_id_type=MESH_ID)
    pl.semaphore_wait(barrier, expected)

    def exchange(number, source_of, buffer, pad, reach, width):
        arrivals, departures = [], []
        for i, (dr, dc) in enumerate((a, b) for a in (-1, 0, 1) for b in (-1, 0, 1)):
            if (dr, dc) == (0, 0) or (dr and not pad):
                continue
            first, span, landing = {
                -1: (0, pad, pad + height), 0: (0, height, pad), 1: (height - pad, pad, 0)
            }[dr]
            left, extent, side = {
                -1: (0, width[1], width[0] + across),
                0: (0, across, width[0]),
                1: (across - width[1], width[1], width[0] - width[1]),
            }[dc]
            copy = pltpu.make_async_remote_copy(
                src_ref=source_of(first, span, left, extent),
                dst_ref=buffer.at[pl.ds(landing, span), pl.ds(side, extent)],
                send_sem=ex_s.at[number, i],
                recv_sem=ex_r.at[number, i],
                device_id=(seg, r + dr * reach, c + dc),
                device_id_type=MESH_ID,
            )
            there, behind = inside[dr * reach, dc], inside[-dr * reach, -dc]
            pl.when(there)(copy.start)
            departures.append((there, copy))
            arrivals.append((behind, copy))

        def arrive():
            for behind, copy in arrivals:
                pl.when(behind)(copy.wait_recv)

        def depart():
            for there, copy in departures:
                pl.when(there)(copy.wait_send)

        return arrive, depart

    def block_of(buffer, pad, margin):
        return lambda first, span, left, extent: buffer.at[
            pl.ds(pad + first, span), pl.ds(margin + left, extent)
        ]

    departs = []
    frame_arrivals = []
    for t in range(steps):
        arrive, depart = exchange(
            t,
            lambda first, span, left, extent, t=t: frames.at[
                seg, t, pl.ds(first, span), pl.ds(left, extent)
            ],
            fp.at[t], 1, 1, (MARGIN, MARGIN),
        )
        frame_arrivals.append(arrive)
        departs.append(depart)

    parts = (2 * seg, 1, 2 * (1 - seg)) if shared else (0, 1, 2)
    carried = range(2) if shared else range(3)

    def slot(a, part, k):
        span = gathered[a].shape[1] // 3
        source = behind_rows[k] if k >= 0 else ahead_rows[-k]
        return gathered[a].at[source, pl.ds(parts[part] * span, span)]

    def ring_copy(a, part, k, sent=True):
        span = gathered[a].shape[1] // 3
        place_of = slot(a, part, k if sent else k + 1)
        start = (9 - 3 * span) // 2 + parts[part] * span
        return pltpu.make_async_remote_copy(
            src_ref=stored[a].at[pl.ds(start, span)] if sent and k == 0 else place_of,
            dst_ref=place_of,
            send_sem=ring_s.at[a, part, k],
            recv_sem=ring_r.at[a, part, k],
            device_id=ahead_id,
            device_id_type=MESH_ID,
        )

    def across_copy(a, k, sent=True):
        piece = slot(a, 0 if sent else 2, k)
        return pltpu.make_async_remote_copy(
            src_ref=piece, dst_ref=piece, send_sem=across_s.at[a, k], recv_sem=across_r.at[a, k],
            device_id=(1 - seg, r, c), device_id_type=MESH_ID,
        )

    def pair_copy(a, part, k, direction):
        piece = slot(a, part, direction * k)
        return pltpu.make_async_remote_copy(
            src_ref=piece, dst_ref=piece, send_sem=pair_s.at[a, part, k],
            recv_sem=pair_r.at[a, part, k], device_id=partner_id, device_id_type=MESH_ID,
        )

    def longer(a):
        return even_core if a == 0 else odd_core

    def guarded(condition, act):
        if condition is None:
            act()
        else:
            pl.when(condition)(act)

    def ring_send(a, part, k):
        guarded(longer(a) if k == half - 1 else None, ring_copy(a, part, k).start)

    def own_send(a):
        for part in carried:
            ring_send(a, part, 0)

    def ring_step(a, k):
        def act():
            for part in carried:
                ring_copy(a, part, k - 1, False).wait_recv()
                if k < half:
                    ring_send(a, part, k)
                if shared and part == 0:
                    across_copy(a, k).start()
                pair_copy(a, part, k, 1).start()

        guarded(longer(a) if k == half else None, act)

    def across_step(a, k):
        def act():
            across_copy(a, k, False).wait_recv()
            pair_copy(a, 2, k, 1).start()

        if shared:
            guarded(longer(a) if k == half else None, act)

    def pair_waits(a):
        shorter = odd_core if a == 0 else even_core
        for k in range(1, half + 1):
            for part in range(3):
                guarded(
                    shorter if k == half else None, pair_copy(a, part, k, -1).wait_recv
                )

    context_steps = list(range(1, half + 1))
    quarter = max(1, half // 4)

    def context_ring(count):
        for _ in range(min(count, len(context_steps))):
            k = context_steps.pop(0)
            for a in (1, 2, 3):
                ring_step(a, k)
            if k > 1:
                for a in (1, 2, 3):
                    across_step(a, k - 1)

    own_send(0)
    for k in range(1, half + 1):
        ring_step(0, k)
        if k > 1:
            across_step(0, k - 1)
        if k == 1:
            for a in (1, 2, 3):
                own_send(a)
        else:
            context_ring(1)
    context_ring(quarter)
    across_step(0, half)

    for copy in locals_:
        copy.wait()
    for arrive in frame_arrivals:
        arrive()
    pair_waits(0)

    bias = cell_b[...].reshape(1, -1)
    per = wc.shape[2]
    frame_sources = channels // per

    def tap_columns(buffer):
        taps = []
        for row in range(height + 2):
            wide = buffer[row].astype(jnp.float32)
            length = wide.shape[0]
            taps.append(
                [
                    pltpu.roll(wide, 1, 0)[MARGIN : MARGIN + across].astype(jnp.bfloat16),
                    buffer[row, MARGIN : MARGIN + across],
                    pltpu.roll(wide, length - 1, 0)[MARGIN : MARGIN + across].astype(
                        jnp.bfloat16
                    ),
                ]
            )
        return taps

    def gate_part(buffer, sources):
        taps = tap_columns(buffer)
        left = jnp.concatenate(
            [
                jnp.concatenate([taps[row + a][b] for row in range(height)], axis=0)
                for a in range(3)
                for b in range(3)
            ],
            axis=1,
        )
        right = jnp.concatenate([wc[s, t] for t in range(9) for s in sources], axis=0)
        return jnp.dot(left, right, preferred_element_type=jnp.float32)

    def update(gates, memory):
        inflow = jax.nn.sigmoid(gates[:, :state])
        forget = jax.nn.sigmoid(gates[:, state : 2 * state])
        output = jax.nn.sigmoid(gates[:, 2 * state : 3 * state])
        fresh = inflow * jnp.tanh(gates[:, 3 * state :])
        memory = fresh if memory is None else forget * memory + fresh
        return (output * jnp.tanh(memory)).astype(jnp.bfloat16), memory

    seen, unseen = range(frame_sources), range(frame_sources, n)
    hidden, memory = update(gate_part(fp.at[0], seen) + bias, None)
    for t in range(1, steps):
        view = hp.at[t - 1]
        for row in range(height):
            view[1 + row, MARGIN : MARGIN + across] = hidden[row * across : (row + 1) * across]
        arrive, depart = exchange(
            steps + t - 1, block_of(view, 1, MARGIN), view, 1, 1, (MARGIN, MARGIN)
        )
        departs.append(depart)
        context_ring(quarter)
        gates = gate_part(fp.at[t], seen) + bias
        context_ring(quarter)
        arrive()
        hidden, memory = update(gates + gate_part(view, unseen), memory)

    feature = hidden
    layers = ((f1, w1, first_b), (f2, w2, second_b), (f3, w3, third_b))
    for i, (buffer, weight, offset) in enumerate(layers):
        spacing, pad = DILATIONS[i], row_pads[i]
        for row in range(height):
            buffer[pad + row, spacing : spacing + across] = feature[
                row * across : (row + 1) * across
            ]
        arrive, depart = exchange(
            2 * steps - 1 + i, block_of(buffer, pad, spacing), buffer, pad,
            spacing // height, (spacing, spacing),
        )
        departs.append(depart)
        if i == 0:
            context_ring(len(context_steps))
            for a in (1, 2, 3):
                across_step(a, half)
        pair_waits(i + 1)
        arrive()
        total = None
        taps = weight.shape[1]
        for t in range(taps):
            a, b = t // 3, t % 3
            left = buffer[a * pad : a * pad + height, b * spacing : b * spacing + across]
            left = left.reshape(height * across, left.shape[-1])
            right = jnp.concatenate([weight[s, t] for s in range(n)], axis=0)
            product = jnp.dot(left, right, preferred_element_type=jnp.float32)
            total = product if total is None else total + product
        result = jnp.maximum(total + offset[...].reshape(1, -1), 0.0)
        if i < 2:
            feature = result.astype(jnp.bfloat16)
    context = (feature.astype(jnp.float32) + result).astype(jnp.bfloat16)
    out[0] = context.reshape(out.shape[1:])

    for depart in departs:
        depart()
    for a in range(4):
        for k in range(half):
            for part in carried:
                guarded(
                    longer(a) if k == half - 1 else None, ring_copy(a, part, k).wait_send
                )
        for k in range(1, half + 1):
            for part in range(3):
                guarded(longer(a) if k == half else None, pair_copy(a, part, k, 1).wait_send)
            if shared:
                guarded(longer(a) if k == half else None, across_copy(a, k).wait_send)


def per_device(n, cols, shared, *args):
    frames, cell_w, cell_b, first_w, first_b, second_w, second_b, third_w, third_b = args
    micro, steps, height, across, channels = frames.shape
    state, width = cell_b.shape[0] // 4, first_b.shape[0]
    row_pads = tuple(height if s // height < n else 0 for s in DILATIONS)

    def slots(weight, pad):
        return pltpu.VMEM((n, 9 if pad else 3) + weight.shape[1:], weight.dtype)

    def field(spacing, pad, depth):
        return pltpu.VMEM((height + 2 * pad, across + 2 * spacing, depth), jnp.bfloat16)

    half = n // 2
    exchanges = 2 * steps - 1 + 3
    dma = pltpu.SemaphoreType.DMA
    anywhere, vmem = pl.BlockSpec(memory_space=pl.ANY), pl.BlockSpec(memory_space=pltpu.VMEM)
    return pl.pallas_call(
        functools.partial(encoder_kernel, n=n, cols=cols, shared=shared, row_pads=row_pads),
        out_shape=jax.ShapeDtypeStruct((1, height, across, width), jnp.bfloat16),
        in_specs=[anywhere, anywhere, vmem, anywhere, vmem, anywhere, vmem, anywhere, vmem],
        out_specs=vmem,
        scratch_shapes=[
            slots(cell_w, 1),
            slots(first_w, row_pads[0]),
            slots(second_w, row_pads[1]),
            slots(third_w, row_pads[2]),
            pltpu.VMEM((steps, height + 2, across + 2 * MARGIN, channels), jnp.bfloat16),
            pltpu.VMEM((steps - 1, height + 2, across + 2 * MARGIN, state), jnp.bfloat16),
            field(DILATIONS[0], row_pads[0], state),
            field(DILATIONS[1], row_pads[1], width),
            field(DILATIONS[2], row_pads[2], width),
            dma((steps + 4,)),
            dma((4, 3, half)),
            dma((4, 3, half)),
            dma((4, half + 1)),
            dma((4, half + 1)),
            dma((4, 3, half + 1)),
            dma((4, 3, half + 1)),
            dma((exchanges, 9)),
            dma((exchanges, 9)),
        ],
        compiler_params=pltpu.CompilerParams(collective_id=0, has_side_effects=True),
    )(
        frames, cell_w, cell_b, first_w, first_b, second_w, second_b,
        third_w, third_b,
    )


def grid_kernel(
    frames, cell_w, cell_b, first_w, first_b, second_w, second_b, third_w, third_b,
    out, wc, w1, w23, fp, hp, f1, f2, f3, biases,
    local_sem, z_sem, y_sem, x_sem, relay_sem, link_sem, twin_s, twin_r, ex_s, ex_r, col_s, col_r,
    *, n,
):
    x, r, c = lax.axis_index("segment"), lax.axis_index("rows"), lax.axis_index("cols")
    steps, height, across, channels = frames.shape[1:]
    state = cell_b.shape[-1] // 4
    planes = n // 2
    reach = planes - 1
    z, y = lax.div(r, 2), lax.rem(r, 2)
    ry = r + 1 - 2 * y
    twin = 1 - c
    even_core, odd_core = c == 0, c == 1

    def run(condition, act):
        if condition is None:
            act()
        else:
            pl.when(condition)(act)

    near_side = jnp.where(z < planes - 1 - z, z, planes - 1 - z)
    long_side = jnp.where(z < planes - 1 - z, 1, -1)

    def other(j):
        paired = j < 2 * near_side
        k = jnp.where(paired, j // 2 + 1, j + 1 - near_side)
        return z + jnp.where(paired, long_side * (1 - 2 * (j % 2)), long_side) * k

    others = [other(j) for j in range(reach)]

    pads = [steps - t for t in range(steps)]
    locals_ = [
        pltpu.make_async_copy(
            cell_w.at[:, :, pl.ds(half * 2 * state, 2 * state)], wc.at[half, r],
            local_sem.at[0],
        )
        for half in range(2)
    ]
    locals_.append(pltpu.make_async_copy(first_w.at[pl.ds(3, 3)], w1.at[r], local_sem.at[1]))
    for half, weight in enumerate((second_w, third_w)):
        locals_.append(
            pltpu.make_async_copy(weight.at[pl.ds(3, 3)], w23.at[half, r], local_sem.at[2])
        )
    for t in range(steps):
        locals_.append(
            pltpu.make_async_copy(
                frames.at[x, t],
                fp.at[t, pl.ds(pads[t], height), pl.ds(MARGIN, across)],
                local_sem.at[3],
            )
        )
    offset = 0
    spans = []
    for vector in (cell_b, first_b, second_b, third_b):
        length = vector.shape[0]
        spans.append((offset, length))
        locals_.append(
            pltpu.make_async_copy(vector, biases.at[pl.ds(offset, length)], local_sem.at[4])
        )
        offset += length
    for copy in locals_:
        copy.start()

    def local_wait(number, ref):
        pltpu.make_async_copy(ref, ref, local_sem.at[number]).wait()

    def row_inside(row):
        return jnp.logical_and(row >= 0, row < n)

    barrier = pltpu.get_barrier_semaphore()
    expected = jnp.int32(2 + reach)
    pl.semaphore_signal(barrier, inc=1, device_id=(1 - x, r, c), device_id_type=MESH_ID)
    pl.semaphore_signal(barrier, inc=1, device_id=(x, r, twin), device_id_type=MESH_ID)
    for plane in others:
        pl.semaphore_signal(
            barrier, inc=1, device_id=(x, 2 * plane + y, c), device_id_type=MESH_ID
        )
    for d in (-1, 1):
        there = row_inside(r + d)
        expected = expected + 2 * there.astype(jnp.int32)

        @pl.when(there)
        def _(d=d):
            for core in (c, twin):
                pl.semaphore_signal(
                    barrier, inc=1, device_id=(x, r + d, core), device_id_type=MESH_ID
                )

    pl.semaphore_wait(barrier, expected)

    depth = wc.shape[3]
    part_rows = 16 if depth % 16 == 0 else depth
    parts = depth // part_rows
    kinds = parts + 2
    first_kind, context_kind = parts, parts + 1
    taps_of = [wc.shape[2]] * parts + [w1.shape[1], w23.shape[2]]
    gates = pl.multiple_of(c * 2 * state, 2 * state)

    def holder(a):
        return odd_core if a == first_kind else None

    def taker(a):
        return even_core if a == first_kind else None

    def carried(a):
        larger = (taps_of[a] + 1) // 2
        return pl.ds((taps_of[a] - larger) * x, larger)

    def only_here(a, there=False):
        larger = (taps_of[a] + 1) // 2
        return pl.ds(larger * (1 - x if there else x), taps_of[a] - larger)

    def everything(a):
        return pl.ds(0, taps_of[a])

    def piece(a, half, s, taps):
        if a < parts:
            return wc.at[half, s, taps, pl.ds(a * part_rows, part_rows)]
        if a == first_kind:
            return w1.at[s, taps]
        return w23.at[half, s, taps]

    def stored(a, taps):
        if a < parts:
            return cell_w.at[taps, pl.ds(a * part_rows, part_rows), pl.ds(gates, 2 * state)]
        return None

    twin_id, beside, opposite = (x, r, twin), (x, ry, c), (1 - x, r, c)
    departures = []

    def remote(source, ref, sent, landed, device):
        return pltpu.make_async_remote_copy(
            src_ref=source, dst_ref=ref, send_sem=sent, recv_sem=landed,
            device_id=device, device_id_type=MESH_ID,
        )

    def send(a, s, taps, landed, device, source=None):
        ref = piece(a, c, s, taps)
        copy = remote(ref if source is None else source, ref, link_sem.at[a], landed, device)
        run(holder(a), copy.start)

    def hand_over(a, s, taps):
        ref = piece(a, c, s, taps)
        run(holder(a), remote(ref, ref, twin_s.at[a], twin_r.at[a], twin_id).start)

    def receive(a, ref, landed):
        run(holder(a), remote(ref, ref, link_sem.at[a], landed, twin_id).wait_recv)

    def z_send(a, j):
        device = (x, 2 * others[j] + y, c)
        send(a, r, carried(a), z_sem.at[a, z], device, stored(a, carried(a)))

    def y_taps(a, j):
        return everything(a) if a < parts and j < 0 else carried(a)

    def relays(a):
        return range(0 if a < parts else -1, reach)

    def own_send(a):
        taps = y_taps(a, -1)
        send(a, r, taps, y_sem.at[a, z], beside, stored(a, taps))

    def z_step(a, j):
        plane = others[j]
        s = 2 * plane + y
        receive(a, piece(a, c, s, carried(a)), z_sem.at[a, plane])
        send(a, s, carried(a), y_sem.at[a, plane], beside)
        send(a, s, only_here(a), x_sem.at[a], opposite)
        hand_over(a, s, carried(a))

    def y_step(a, j):
        plane = z if j < 0 else others[j]
        s = 2 * plane + 1 - y
        receive(a, piece(a, c, s, y_taps(a, j)), y_sem.at[a, plane])
        if j in relays(a):
            send(a, s, only_here(a), relay_sem.at[a], opposite)
        hand_over(a, s, y_taps(a, j))

    def several(a, half, count, taps):
        if a < parts:
            return wc.at[half, pl.ds(0, count), taps, pl.ds(a * part_rows, part_rows)]
        if a == first_kind:
            return w1.at[pl.ds(0, count), taps]
        return w23.at[half, pl.ds(0, count), taps]

    def x_step(a, _):
        receive(a, several(a, c, reach, only_here(a, True)), x_sem.at[a])
        for plane in others:
            hand_over(a, 2 * plane + y, only_here(a, True))

    def relay_step(a, _):
        receive(a, several(a, c, len(relays(a)), only_here(a, True)), relay_sem.at[a])
        for j in relays(a):
            plane = z if j < 0 else others[j]
            hand_over(a, 2 * plane + 1 - y, only_here(a, True))

    def twin_waits(a):
        ref = several(a, twin, n - 1, everything(a))
        run(taker(a), remote(ref, ref, twin_s.at[a], twin_r.at[a], twin_id).wait_recv)

    def sent_waits(a):
        ref = several(a, c, n - 1, everything(a))
        for sem in (link_sem, twin_s):
            run(holder(a), remote(ref, ref, sem.at[a], twin_r.at[a], twin_id).wait_send)

    for a in range(parts):
        for j in range(reach):
            z_send(a, j)
        own_send(a)

    side = across + MARGIN
    rims = sum(pads)
    for d in (-1, 0, 1):
        there = row_inside(r + d) if d else None

        def rim(act, d=d):
            for t in range(steps):
                pad = pads[t]
                first, span, landing = {
                    -1: (0, pad, pad + height), 0: (0, height, pad), 1: (height - pad, pad, 0)
                }[d]
                for core in (c, twin):
                    if core is c and d == 0:
                        continue
                    if core is c:
                        left, extent, place = 0, across, MARGIN
                    else:
                        left = pl.multiple_of((1 - c) * (across - MARGIN), 16)
                        extent, place = MARGIN, pl.multiple_of(c * (across + MARGIN), 16)
                    act(
                        remote(
                            frames.at[x, t, pl.ds(first, span), pl.ds(left, extent)],
                            fp.at[t, pl.ds(landing, span), pl.ds(place, extent)],
                            ex_s.at[d + 1], ex_r.at[d + 1], (x, r + d, core),
                        )
                    )

        run(there, lambda: rim(lambda copy: copy.start()))

    def rim_ref(d):
        if d == 0:
            return fp.at[:, pl.ds(0, height), pl.ds(0, MARGIN)]
        return fp.at[0, pl.ds(0, rims), pl.ds(0, side)]

    def rims_arrive():
        for d in (-1, 0, 1):
            ref = rim_ref(d)
            copy = remote(ref, ref, ex_s.at[d + 1], ex_r.at[d + 1], twin_id)
            run(row_inside(r - d) if d else None, copy.wait_recv)

    def rims_leave():
        for d in (-1, 0, 1):
            ref = rim_ref(d)
            copy = remote(ref, ref, ex_s.at[d + 1], ex_r.at[d + 1], twin_id)
            run(row_inside(r + d) if d else None, copy.wait_send)

    local_wait(1, w1.at[r])
    local_wait(2, w23.at[:, r])

    def context_sends(a):
        for j in range(reach):
            z_send(a, j)
        own_send(a)

    for t in range(steps):
        pad = pads[t]
        total_rows = height + 2 * pad

        def blank(ref, first, count, left, extent):
            ref[first : first + count, left : left + extent] = jnp.zeros(
                (count, extent, ref.shape[-1]), ref.dtype
            )

        @pl.when(r == 0)
        def _(t=t, pad=pad):
            blank(fp.at[t], 0, pad, 0, across + 2 * MARGIN)

        @pl.when(r == n - 1)
        def _(t=t, pad=pad):
            blank(fp.at[t], pad + height, pad, 0, across + 2 * MARGIN)

        @pl.when(even_core)
        def _(t=t, total_rows=total_rows):
            blank(fp.at[t], 0, total_rows, 0, MARGIN)

        @pl.when(odd_core)
        def _(t=t, total_rows=total_rows):
            blank(fp.at[t], 0, total_rows, MARGIN + across, MARGIN)

    for ref, margin in ((f1, DILATIONS[0]), (f2, DILATIONS[1])):
        blank(ref, 0, ref.shape[0], 0, margin)
        blank(ref, 0, ref.shape[0], margin + 2 * across, margin)
    for ref, margin in [(hp.at[t], MARGIN) for t in range(steps - 1)]:
        @pl.when(even_core)
        def _(ref=ref, margin=margin):
            blank(ref, 0, ref.shape[0], 0, margin)

        @pl.when(odd_core)
        def _(ref=ref, margin=margin):
            blank(ref, 0, ref.shape[0], margin + across, margin)

    plan = []
    for a in range(kinds):
        start, pace, hop = TIMES[min(a, 1)] if a < parts else TIMES[a - parts + 2]
        if a >= parts:
            plan.append((SENDS, lambda a, _: context_sends(a), a, 0))
        plan.append((start + 0.6, y_step, a, -1))
        for k in range(reach):
            there = start + pace * k
            plan.append((there, z_step, a, k))
            plan.append((there + hop, y_step, a, k))
        plan.append((there + hop - 0.1, x_step, a, 0))
        plan.append((there + 2 * hop, relay_step, a, 0))
    plan.sort(key=lambda entry: entry[0])
    cell_done = max(i for i, entry in enumerate(plan) if entry[2] < parts)
    first_done = max(i for i, entry in enumerate(plan) if entry[2] <= first_kind)
    marks = [cell_done + 1, first_done + 1, len(plan)]
    taken = [0]

    def advance(mark):
        while taken[0] < mark:
            _, step, a, k = plan[taken[0]]
            step(a, k)
            taken[0] += 1

    advance(marks[0])
    local_wait(0, wc.at[:, r])
    local_wait(3, fp.at[:, pl.ds(0, height), pl.ds(0, across)])
    local_wait(4, biases)
    rims_arrive()
    for a in range(parts):
        twin_waits(a)

    cell_bias, first_bias, second_bias, third_bias = [
        biases[at : at + length].reshape(1, -1) for at, length in spans
    ]
    per = wc.shape[3]
    frame_sources = channels // per

    def tap_columns(buffer, count):
        taps = []
        for row in range(count):
            wide_row = buffer[row].astype(jnp.float32)
            length = wide_row.shape[0]
            taps.append(
                [
                    pltpu.roll(wide_row, 1, 0)[MARGIN : MARGIN + across].astype(jnp.bfloat16),
                    buffer[row, MARGIN : MARGIN + across],
                    pltpu.roll(wide_row, length - 1, 0)[MARGIN : MARGIN + across].astype(
                        jnp.bfloat16
                    ),
                ]
            )
        return taps

    def columns_of(buffer, count):
        taps = tap_columns(buffer, count + 2)
        return jnp.concatenate(
            [
                jnp.concatenate([taps[row + a][b] for row in range(count)], axis=0)
                for a in range(3)
                for b in range(3)
            ],
            axis=1,
        )

    def gate_part(left, sources):
        return [
            jnp.dot(
                left,
                jnp.concatenate([wc[half, s, t] for t in range(9) for s in sources], axis=0),
                preferred_element_type=jnp.float32,
            )
            for half in range(2)
        ]

    def update(gates, memory):
        inflow = jax.nn.sigmoid(gates[0][:, :state])
        output = jax.nn.sigmoid(gates[1][:, :state])
        fresh = inflow * jnp.tanh(gates[1][:, state:])
        if memory is None:
            memory = fresh
        else:
            memory = jax.nn.sigmoid(gates[0][:, state:]) * memory + fresh
        return (output * jnp.tanh(memory)).astype(jnp.bfloat16), memory

    swaps = []

    def exchange_columns(number, buffer, margin):
        sent = pl.multiple_of((1 - c) * across + c * margin, 16)
        landing = pl.multiple_of(c * (margin + across), 16)
        copy = pltpu.make_async_remote_copy(
            src_ref=buffer.at[:, pl.ds(sent, margin)],
            dst_ref=buffer.at[:, pl.ds(landing, margin)],
            send_sem=col_s.at[number],
            recv_sem=col_r.at[number],
            device_id=(x, r, twin),
            device_id_type=MESH_ID,
        )
        copy.start()
        departures.append(copy)
        return copy

    seen, unseen = range(frame_sources), range(frame_sources, n)
    counts = [height + 2 * (steps - 1 - t) for t in range(steps)]
    lefts = jnp.concatenate(
        [columns_of(fp.at[t], counts[t]) for t in range(steps)], axis=0
    )
    frame_gates = gate_part(lefts, seen)
    start = 0
    memory = None
    for t in range(steps):
        length = counts[t] * across
        gates = [
            part[start : start + length] + cell_bias[:, half * 2 * state : (half + 1) * 2 * state]
            for half, part in enumerate(frame_gates)
        ]
        start += length
        if t:
            swaps[-1].wait_recv()
            extra = gate_part(columns_of(hp.at[t - 1], counts[t]), unseen)
            gates = [one + more for one, more in zip(gates, extra)]
            memory = memory[across : memory.shape[0] - across]
        hidden, memory = update(gates, memory)
        if t == steps - 1:
            break
        view = hp.at[t]
        outside = steps - 1 - t
        for row in range(counts[t]):
            value = hidden[row * across : (row + 1) * across]
            if row < outside or row >= counts[t] - outside:
                place = r * height + row - outside
                valid = jnp.logical_and(place >= 0, place < n * height)
                value = jnp.where(valid, value, jnp.zeros_like(value))
            view[row, MARGIN : MARGIN + across] = value
        swaps.append(exchange_columns(t, view, MARGIN))


    def product(left, weight):
        return jnp.dot(
            left.reshape(-1, left.shape[-1]), weight, preferred_element_type=jnp.float32
        )

    margin = DILATIONS[0]
    block = pl.ds(pl.multiple_of(margin + c * across, 16), across)
    f1[:, block] = hidden.reshape(height, across, state)
    swap = pltpu.make_async_remote_copy(
        src_ref=f1.at[:, block], dst_ref=f1.at[:, block], send_sem=col_s.at[steps - 1],
        recv_sem=col_r.at[steps - 1], device_id=(x, r, twin), device_id_type=MESH_ID,
    )
    swap.start()
    departures.append(swap)
    advance(marks[1])
    twin_waits(first_kind)
    swap.wait_recv()

    def convolve(buffer, margin, weight, offset):
        total = None
        for b in range(3):
            more = product(buffer[:, b * margin : b * margin + 2 * across], weight(b))
            total = more if total is None else total + more
        return jnp.maximum(total + offset, 0.0).astype(jnp.bfloat16)

    first = convolve(
        f1, margin, lambda b: jnp.concatenate([w1[s, b] for s in range(n)], axis=0), first_bias
    )
    margin = DILATIONS[1]
    f2[:, margin : margin + 2 * across] = first.reshape(height, 2 * across, -1)
    advance(marks[2])
    for a in range(parts):
        sent_waits(a)
    rims_leave()
    twin_waits(context_kind)
    second = convolve(
        f2, margin, lambda b: jnp.concatenate([w23[0, s, b] for s in range(n)], axis=0),
        second_bias,
    )
    second = second.reshape(height, 2, across, -1)
    for col in range(2):
        f3[col] = second[:, col]

    def last(b):
        return jnp.concatenate([w23[1, s, b] for s in range(n)], axis=0)

    feature = f3[c].reshape(height * across, -1)
    total = product(feature, last(1)) + product(f3[twin], last(2 - 2 * c))
    result = jnp.maximum(total + third_bias, 0.0)
    context = (feature.astype(jnp.float32) + result).astype(jnp.bfloat16)
    out[0] = context.reshape(out.shape[1:])
    sent_waits(first_kind)
    sent_waits(context_kind)
    for copy in departures:
        copy.wait_send()


def grid_device(n, *args):
    frames, cell_w, cell_b, first_w, first_b, second_w, second_b, third_w, third_b = args
    micro, steps, height, across, channels = frames.shape
    state, width = cell_b.shape[0] // 4, first_b.shape[0]
    depth = cell_w.shape[1]
    kinds = (depth // 16 if depth % 16 == 0 else 1) + 2
    dma, bf16 = pltpu.SemaphoreType.DMA, jnp.bfloat16
    anywhere, vmem = pl.BlockSpec(memory_space=pl.ANY), pl.BlockSpec(memory_space=pltpu.VMEM)
    return pl.pallas_call(
        functools.partial(grid_kernel, n=n),
        out_shape=jax.ShapeDtypeStruct((1, height, across, width), bf16),
        in_specs=[anywhere] * 9,
        out_specs=vmem,
        scratch_shapes=[
            pltpu.VMEM((2, n, 9, cell_w.shape[1], 2 * state), bf16),
            pltpu.VMEM((n, 3) + first_w.shape[1:], bf16),
            pltpu.VMEM((2, n, 3) + second_w.shape[1:], bf16),
            pltpu.VMEM((steps, height + 2 * steps, across + 2 * MARGIN, channels), bf16),
            pltpu.VMEM((steps - 1, height + 2 * (steps - 1), across + 2 * MARGIN, state), bf16),
            pltpu.VMEM((height, 2 * (across + DILATIONS[0]), state), bf16),
            pltpu.VMEM((height, 2 * (across + DILATIONS[1]), width), bf16),
            pltpu.VMEM((2, height, across, width), bf16),
            pltpu.VMEM((sum(v.shape[0] for v in (cell_b, first_b, second_b, third_b)),), jnp.float32),
            dma((5,)),
            dma((kinds, n // 2)),
            dma((kinds, n // 2)),
            dma((kinds,)),
            dma((kinds,)),
            dma((kinds,)),
            dma((kinds,)),
            dma((kinds,)),
            dma((3,)),
            dma((3,)),
            dma((steps,)),
            dma((steps,)),
        ],
        compiler_params=pltpu.CompilerParams(collective_id=1, has_side_effects=True),
    )(*args)


def fits_grid(mesh, frames):
    n, cols = mesh.shape["rows"], mesh.shape["cols"]
    micro, steps, height, across, channels = frames.shape
    return (
        mesh.shape["segment"] == 2 and cols == 2 and n % 2 == 0 and n > 2
        and min(DILATIONS) // height >= n and DILATIONS[-1] == across
        and max(DILATIONS[:-1]) <= across and steps <= height
    )


def solution(mesh):
    kernels = P(None, "rows", None)
    placed = (
        P(None, None, "rows", "cols", None),
        kernels, P(), kernels, P(), kernels, P(), kernels, P(),
    )
    n, cols = mesh.shape["rows"], mesh.shape["cols"]

    def on_device(*args):
        if fits_grid(mesh, args[0]):
            return grid_device(n, *args)
        return per_device(n, cols, mesh.shape["segment"] == 2, *args)

    return jax.shard_map(
        on_device,
        mesh=mesh,
        in_specs=placed,
        out_specs=P("segment", "rows", "cols", None),
        check_vma=False,
    )
```

```python
import functools

import jax
import jax.numpy as jnp
from jax import lax
from jax.experimental import pallas as pl
from jax.experimental.pallas import tpu as pltpu
from jax.sharding import PartitionSpec as P

DILATIONS = (16, 32, 64)
MESH_ID = pl.DeviceIdType.MESH
MARGIN = 16
CELL = (3.2, 1.3, 1.0, 2.8)
SENDS = (0.2, 0.3, 0.4)
CONTEXTS = ((4.0, 1.0, 3.2), (8.0, 1.0, 3.2), (10.0, 1.0, 3.2))
PAUSE = 17.0
DIRECT = (99, 2)


def encoder_kernel(
    frames, cell_w, cell_b, first_w, first_b, second_w, second_b, third_w, third_b,
    out, wc, w1, w2, w3, fp, hp, f1, f2, f3,
    local_sem, ring_s, ring_r, across_s, across_r, pair_s, pair_r, ex_s, ex_r, *, n, cols, shared, row_pads,
):
    seg, r, c = lax.axis_index("segment"), lax.axis_index("rows"), lax.axis_index("cols")
    steps, height, across, channels = frames.shape[1:]
    state = cell_b.shape[-1] // 4
    half = n // 2
    odd = lax.rem(c, 2)
    even_core, odd_core = odd == 0, odd == 1
    sign = 1 - 2 * odd
    parity, pair = lax.rem(r, 2), lax.div(r, 2)
    place = pair + parity * (n - 1 - 2 * pair)

    def rows_at(position):
        upper = lax.div(position, half)
        return 2 * position + upper * (2 * n - 1 - 4 * position)

    behind_rows = [r] + [rows_at(lax.rem(place - sign * k + n, n)) for k in range(1, half + 1)]
    ahead_rows = [r] + [rows_at(lax.rem(place + sign * k + n, n)) for k in range(1, half + 1)]
    following, preceding = ahead_rows[1], behind_rows[1]
    partner = c + 1 - 2 * odd
    ahead_id, partner_id = (seg, following, c), (seg, r, partner)

    reaches = sorted({1} | {s // height for s, pad in zip(DILATIONS, row_pads) if pad})
    offsets = [(0, -1), (0, 1)] + [
        (d * reach, dc) for reach in reaches for d in (-1, 1) for dc in (-1, 0, 1)
    ]

    def present(dr, dc):
        row, col = r + dr, c + dc
        return jnp.logical_and(
            jnp.logical_and(row >= 0, row < n), jnp.logical_and(col >= 0, col < cols)
        )

    inside = {offset: present(*offset) for offset in offsets}

    locals_ = []
    for t in range(steps):
        locals_.append(
            pltpu.make_async_copy(
                frames.at[seg, t],
                fp.at[t, pl.ds(1, height), pl.ds(MARGIN, across)],
                local_sem.at[t],
            )
        )
    stored = (cell_w, first_w, second_w, third_w)
    gathered = (wc, w1, w2, w3)
    own = []
    for ref, whole in zip(stored, gathered):
        taps = whole.shape[1]
        own.append(ref.at[pl.ds((9 - taps) // 2, taps)])
    for a in range(4):
        locals_.append(
            pltpu.make_async_copy(own[a], gathered[a].at[r], local_sem.at[steps + a])
        )
    for t in range(steps):
        fp[t] = jnp.zeros(fp.shape[1:], fp.dtype)
    for t in range(hp.shape[0]):
        hp[t] = jnp.zeros(hp.shape[1:], hp.dtype)
    for buffer in (f1, f2, f3):
        buffer[...] = jnp.zeros(buffer.shape, buffer.dtype)
    for copy in locals_:
        copy.start()

    barrier = pltpu.get_barrier_semaphore()
    expected = jnp.int32(2)
    for target in (following, preceding):
        pl.semaphore_signal(barrier, inc=1, device_id=(seg, target, c), device_id_type=MESH_ID)
    for dr, dc in offsets:
        there = inside[dr, dc]
        expected = expected + there.astype(jnp.int32)

        @pl.when(there)
        def _():
            pl.semaphore_signal(
                barrier, inc=1, device_id=(seg, r + dr, c + dc), device_id_type=MESH_ID
            )

    if shared:
        expected = expected + 1
        pl.semaphore_signal(barrier, inc=1, device_id=(1 - seg, r, c), device_id_type=MESH_ID)
    pl.semaphore_wait(barrier, expected)

    def exchange(number, source_of, buffer, pad, reach, width):
        arrivals, departures = [], []
        for i, (dr, dc) in enumerate((a, b) for a in (-1, 0, 1) for b in (-1, 0, 1)):
            if (dr, dc) == (0, 0) or (dr and not pad):
                continue
            first, span, landing = {
                -1: (0, pad, pad + height), 0: (0, height, pad), 1: (height - pad, pad, 0)
            }[dr]
            left, extent, side = {
                -1: (0, width[1], width[0] + across),
                0: (0, across, width[0]),
                1: (across - width[1], width[1], width[0] - width[1]),
            }[dc]
            copy = pltpu.make_async_remote_copy(
                src_ref=source_of(first, span, left, extent),
                dst_ref=buffer.at[pl.ds(landing, span), pl.ds(side, extent)],
                send_sem=ex_s.at[number, i],
                recv_sem=ex_r.at[number, i],
                device_id=(seg, r + dr * reach, c + dc),
                device_id_type=MESH_ID,
            )
            there, behind = inside[dr * reach, dc], inside[-dr * reach, -dc]
            pl.when(there)(copy.start)
            departures.append((there, copy))
            arrivals.append((behind, copy))

        def arrive():
            for behind, copy in arrivals:
                pl.when(behind)(copy.wait_recv)

        def depart():
            for there, copy in departures:
                pl.when(there)(copy.wait_send)

        return arrive, depart

    def block_of(buffer, pad, margin):
        return lambda first, span, left, extent: buffer.at[
            pl.ds(pad + first, span), pl.ds(margin + left, extent)
        ]

    departs = []
    frame_arrivals = []
    for t in range(steps):
        arrive, depart = exchange(
            t,
            lambda first, span, left, extent, t=t: frames.at[
                seg, t, pl.ds(first, span), pl.ds(left, extent)
            ],
            fp.at[t], 1, 1, (MARGIN, MARGIN),
        )
        frame_arrivals.append(arrive)
        departs.append(depart)

    parts = (2 * seg, 1, 2 * (1 - seg)) if shared else (0, 1, 2)
    carried = range(2) if shared else range(3)

    def slot(a, part, k):
        span = gathered[a].shape[1] // 3
        source = behind_rows[k] if k >= 0 else ahead_rows[-k]
        return gathered[a].at[source, pl.ds(parts[part] * span, span)]

    def ring_copy(a, part, k, sent=True):
        span = gathered[a].shape[1] // 3
        place_of = slot(a, part, k if sent else k + 1)
        start = (9 - 3 * span) // 2 + parts[part] * span
        return pltpu.make_async_remote_copy(
            src_ref=stored[a].at[pl.ds(start, span)] if sent and k == 0 else place_of,
            dst_ref=place_of,
            send_sem=ring_s.at[a, part, k],
            recv_sem=ring_r.at[a, part, k],
            device_id=ahead_id,
            device_id_type=MESH_ID,
        )

    def across_copy(a, k, sent=True):
        piece = slot(a, 0 if sent else 2, k)
        return pltpu.make_async_remote_copy(
            src_ref=piece, dst_ref=piece, send_sem=across_s.at[a, k], recv_sem=across_r.at[a, k],
            device_id=(1 - seg, r, c), device_id_type=MESH_ID,
        )

    def pair_copy(a, part, k, direction):
        piece = slot(a, part, direction * k)
        return pltpu.make_async_remote_copy(
            src_ref=piece, dst_ref=piece, send_sem=pair_s.at[a, part, k],
            recv_sem=pair_r.at[a, part, k], device_id=partner_id, device_id_type=MESH_ID,
        )

    def longer(a):
        return even_core if a == 0 else odd_core

    def guarded(condition, act):
        if condition is None:
            act()
        else:
            pl.when(condition)(act)

    def ring_send(a, part, k):
        guarded(longer(a) if k == half - 1 else None, ring_copy(a, part, k).start)

    def own_send(a):
        for part in carried:
            ring_send(a, part, 0)

    def ring_step(a, k):
        def act():
            for part in carried:
                ring_copy(a, part, k - 1, False).wait_recv()
                if k < half:
                    ring_send(a, part, k)
                if shared and part == 0:
                    across_copy(a, k).start()
                pair_copy(a, part, k, 1).start()

        guarded(longer(a) if k == half else None, act)

    def across_step(a, k):
        def act():
            across_copy(a, k, False).wait_recv()
            pair_copy(a, 2, k, 1).start()

        if shared:
            guarded(longer(a) if k == half else None, act)

    def pair_waits(a):
        shorter = odd_core if a == 0 else even_core
        for k in range(1, half + 1):
            for part in range(3):
                guarded(
                    shorter if k == half else None, pair_copy(a, part, k, -1).wait_recv
                )

    context_steps = list(range(1, half + 1))
    quarter = max(1, half // 4)

    def context_ring(count):
        for _ in range(min(count, len(context_steps))):
            k = context_steps.pop(0)
            for a in (1, 2, 3):
                ring_step(a, k)
            if k > 1:
                for a in (1, 2, 3):
                    across_step(a, k - 1)

    own_send(0)
    for k in range(1, half + 1):
        ring_step(0, k)
        if k > 1:
            across_step(0, k - 1)
        if k == 1:
            for a in (1, 2, 3):
                own_send(a)
        else:
            context_ring(1)
    context_ring(quarter)
    across_step(0, half)

    for copy in locals_:
        copy.wait()
    for arrive in frame_arrivals:
        arrive()
    pair_waits(0)

    bias = cell_b[...].reshape(1, -1)
    per = wc.shape[2]
    frame_sources = channels // per

    def tap_columns(buffer):
        taps = []
        for row in range(height + 2):
            wide = buffer[row].astype(jnp.float32)
            length = wide.shape[0]
            taps.append(
                [
                    pltpu.roll(wide, 1, 0)[MARGIN : MARGIN + across].astype(jnp.bfloat16),
                    buffer[row, MARGIN : MARGIN + across],
                    pltpu.roll(wide, length - 1, 0)[MARGIN : MARGIN + across].astype(
                        jnp.bfloat16
                    ),
                ]
            )
        return taps

    def gate_part(buffer, sources):
        taps = tap_columns(buffer)
        left = jnp.concatenate(
            [
                jnp.concatenate([taps[row + a][b] for row in range(height)], axis=0)
                for a in range(3)
                for b in range(3)
            ],
            axis=1,
        )
        right = jnp.concatenate([wc[s, t] for t in range(9) for s in sources], axis=0)
        return jnp.dot(left, right, preferred_element_type=jnp.float32)

    def update(gates, memory):
        inflow = jax.nn.sigmoid(gates[:, :state])
        forget = jax.nn.sigmoid(gates[:, state : 2 * state])
        output = jax.nn.sigmoid(gates[:, 2 * state : 3 * state])
        fresh = inflow * jnp.tanh(gates[:, 3 * state :])
        memory = fresh if memory is None else forget * memory + fresh
        return (output * jnp.tanh(memory)).astype(jnp.bfloat16), memory

    seen, unseen = range(frame_sources), range(frame_sources, n)
    hidden, memory = update(gate_part(fp.at[0], seen) + bias, None)
    for t in range(1, steps):
        view = hp.at[t - 1]
        for row in range(height):
            view[1 + row, MARGIN : MARGIN + across] = hidden[row * across : (row + 1) * across]
        arrive, depart = exchange(
            steps + t - 1, block_of(view, 1, MARGIN), view, 1, 1, (MARGIN, MARGIN)
        )
        departs.append(depart)
        context_ring(quarter)
        gates = gate_part(fp.at[t], seen) + bias
        context_ring(quarter)
        arrive()
        hidden, memory = update(gates + gate_part(view, unseen), memory)

    feature = hidden
    layers = ((f1, w1, first_b), (f2, w2, second_b), (f3, w3, third_b))
    for i, (buffer, weight, offset) in enumerate(layers):
        spacing, pad = DILATIONS[i], row_pads[i]
        for row in range(height):
            buffer[pad + row, spacing : spacing + across] = feature[
                row * across : (row + 1) * across
            ]
        arrive, depart = exchange(
            2 * steps - 1 + i, block_of(buffer, pad, spacing), buffer, pad,
            spacing // height, (spacing, spacing),
        )
        departs.append(depart)
        if i == 0:
            context_ring(len(context_steps))
            for a in (1, 2, 3):
                across_step(a, half)
        pair_waits(i + 1)
        arrive()
        total = None
        taps = weight.shape[1]
        for t in range(taps):
            a, b = t // 3, t % 3
            left = buffer[a * pad : a * pad + height, b * spacing : b * spacing + across]
            left = left.reshape(height * across, left.shape[-1])
            right = jnp.concatenate([weight[s, t] for s in range(n)], axis=0)
            product = jnp.dot(left, right, preferred_element_type=jnp.float32)
            total = product if total is None else total + product
        result = jnp.maximum(total + offset[...].reshape(1, -1), 0.0)
        if i < 2:
            feature = result.astype(jnp.bfloat16)
    context = (feature.astype(jnp.float32) + result).astype(jnp.bfloat16)
    out[0] = context.reshape(out.shape[1:])

    for depart in departs:
        depart()
    for a in range(4):
        for k in range(half):
            for part in carried:
                guarded(
                    longer(a) if k == half - 1 else None, ring_copy(a, part, k).wait_send
                )
        for k in range(1, half + 1):
            for part in range(3):
                guarded(longer(a) if k == half else None, pair_copy(a, part, k, 1).wait_send)
            if shared:
                guarded(longer(a) if k == half else None, across_copy(a, k).wait_send)


def per_device(n, cols, shared, *args):
    frames, cell_w, cell_b, first_w, first_b, second_w, second_b, third_w, third_b = args
    micro, steps, height, across, channels = frames.shape
    state, width = cell_b.shape[0] // 4, first_b.shape[0]
    row_pads = tuple(height if s // height < n else 0 for s in DILATIONS)

    def slots(weight, pad):
        return pltpu.VMEM((n, 9 if pad else 3) + weight.shape[1:], weight.dtype)

    def field(spacing, pad, depth):
        return pltpu.VMEM((height + 2 * pad, across + 2 * spacing, depth), jnp.bfloat16)

    half = n // 2
    exchanges = 2 * steps - 1 + 3
    dma = pltpu.SemaphoreType.DMA
    anywhere, vmem = pl.BlockSpec(memory_space=pl.ANY), pl.BlockSpec(memory_space=pltpu.VMEM)
    return pl.pallas_call(
        functools.partial(encoder_kernel, n=n, cols=cols, shared=shared, row_pads=row_pads),
        out_shape=jax.ShapeDtypeStruct((1, height, across, width), jnp.bfloat16),
        in_specs=[anywhere, anywhere, vmem, anywhere, vmem, anywhere, vmem, anywhere, vmem],
        out_specs=vmem,
        scratch_shapes=[
            slots(cell_w, 1),
            slots(first_w, row_pads[0]),
            slots(second_w, row_pads[1]),
            slots(third_w, row_pads[2]),
            pltpu.VMEM((steps, height + 2, across + 2 * MARGIN, channels), jnp.bfloat16),
            pltpu.VMEM((steps - 1, height + 2, across + 2 * MARGIN, state), jnp.bfloat16),
            field(DILATIONS[0], row_pads[0], state),
            field(DILATIONS[1], row_pads[1], width),
            field(DILATIONS[2], row_pads[2], width),
            dma((steps + 4,)),
            dma((4, 3, half)),
            dma((4, 3, half)),
            dma((4, half + 1)),
            dma((4, half + 1)),
            dma((4, 3, half + 1)),
            dma((4, 3, half + 1)),
            dma((exchanges, 9)),
            dma((exchanges, 9)),
        ],
        compiler_params=pltpu.CompilerParams(collective_id=0, has_side_effects=True),
    )(
        frames, cell_w, cell_b, first_w, first_b, second_w, second_b,
        third_w, third_b,
    )


def grid_kernel(
    frames, cell_w, cell_b, first_w, first_b, second_w, second_b, third_w, third_b,
    out, wc, w1, w23, fp, hp, f1, f2, f3, biases,
    local_sem, z_sem, y_sem, x_sem, relay_sem, link_sem, twin_s, twin_r, ex_s, ex_r, col_s, col_r,
    *, n,
):
    x, r, c = lax.axis_index("segment"), lax.axis_index("rows"), lax.axis_index("cols")
    steps, height, across, channels = frames.shape[1:]
    state = cell_b.shape[-1] // 4
    planes = n // 2
    reach = planes - 1
    z, y = lax.div(r, 2), lax.rem(r, 2)
    ry = r + 1 - 2 * y
    twin = 1 - c
    even_core, odd_core = c == 0, c == 1

    def run(condition, act):
        if condition is None:
            act()
        else:
            pl.when(condition)(act)

    near_side = jnp.where(z < planes - 1 - z, z, planes - 1 - z)
    long_side = jnp.where(z < planes - 1 - z, 1, -1)

    def other(j):
        paired = j < 2 * near_side
        k = jnp.where(paired, j // 2 + 1, j + 1 - near_side)
        return z + jnp.where(paired, long_side * (1 - 2 * (j % 2)), long_side) * k

    others = [other(j) for j in range(reach)]

    pads = [steps - t for t in range(steps)]
    locals_ = [
        pltpu.make_async_copy(
            cell_w.at[:, :, pl.ds(half * 2 * state, 2 * state)], wc.at[half, r],
            local_sem.at[0],
        )
        for half in range(2)
    ]
    locals_.append(pltpu.make_async_copy(first_w.at[pl.ds(3, 3)], w1.at[r], local_sem.at[1]))
    for half, weight in enumerate((second_w, third_w)):
        locals_.append(
            pltpu.make_async_copy(weight.at[pl.ds(3, 3)], w23.at[half, r], local_sem.at[2])
        )
    for t in range(steps):
        locals_.append(
            pltpu.make_async_copy(
                frames.at[x, t],
                fp.at[t, pl.ds(pads[t], height), pl.ds(MARGIN, across)],
                local_sem.at[3],
            )
        )
    offset = 0
    spans = []
    for vector in (cell_b, first_b, second_b, third_b):
        length = vector.shape[0]
        spans.append((offset, length))
        locals_.append(
            pltpu.make_async_copy(vector, biases.at[pl.ds(offset, length)], local_sem.at[4])
        )
        offset += length
    for copy in locals_:
        copy.start()

    def local_wait(number, ref):
        pltpu.make_async_copy(ref, ref, local_sem.at[number]).wait()

    def row_inside(row):
        return jnp.logical_and(row >= 0, row < n)

    barrier = pltpu.get_barrier_semaphore()
    expected = jnp.int32(2 + reach)
    pl.semaphore_signal(barrier, inc=1, device_id=(1 - x, r, c), device_id_type=MESH_ID)
    pl.semaphore_signal(barrier, inc=1, device_id=(x, r, twin), device_id_type=MESH_ID)
    for plane in others:
        pl.semaphore_signal(
            barrier, inc=1, device_id=(x, 2 * plane + y, c), device_id_type=MESH_ID
        )
    for d in (-1, 1):
        there = row_inside(r + d)
        expected = expected + 2 * there.astype(jnp.int32)

        @pl.when(there)
        def _(d=d):
            for core in (c, twin):
                pl.semaphore_signal(
                    barrier, inc=1, device_id=(x, r + d, core), device_id_type=MESH_ID
                )

    pl.semaphore_wait(barrier, expected)

    depth = wc.shape[3]
    part_rows = 16 if depth % 16 == 0 else depth
    parts = [
        (half, pl.ds(first, part_rows)) for half in range(2) for first in range(0, depth, part_rows)
    ]
    cells = [("cell", a) for a in range(len(parts))]
    contexts = [("context", a) for a in range(3)]

    def taps_of(kind):
        return wc.shape[2] if kind[0] == "cell" else w1.shape[1]

    def carried(kind):
        larger = (taps_of(kind) + 1) // 2
        return (taps_of(kind) - larger) * x, larger

    def only_here(kind, there=False):
        larger = (taps_of(kind) + 1) // 2
        return larger * (1 - x if there else x), taps_of(kind) - larger

    def everything(kind):
        return 0, taps_of(kind)

    def shards(kind, s, taps):
        taps = pl.ds(*taps)
        if kind[0] == "cell":
            half, rows = parts[kind[1]]
            return wc.at[half, s, taps, rows]
        if kind[1] == 0:
            return w1.at[s, taps]
        return w23.at[kind[1] - 1, s, taps]

    def several(kind, count, taps):
        return shards(kind, pl.ds(0, count), taps)

    def stored(kind, taps):
        if kind[0] == "cell":
            half, rows = parts[kind[1]]
            return cell_w.at[pl.ds(*taps), rows, pl.ds(half * 2 * state, 2 * state)]
        whole = (first_w, second_w, third_w)[kind[1]]
        return whole.at[pl.ds((whole.shape[0] - taps_of(kind)) // 2 + taps[0], taps[1])]

    twin_id, beside, opposite = (x, r, twin), (x, ry, c), (1 - x, r, c)
    departures = []

    def remote(source, ref, sent, landed, device):
        return pltpu.make_async_remote_copy(
            src_ref=source, dst_ref=ref, send_sem=sent, recv_sem=landed,
            device_id=device, device_id_type=MESH_ID,
        )

    def send(kind, s, taps, way, landed, device, own=False):
        ref = shards(kind, s, taps)
        source = stored(kind, taps) if own else ref
        remote(source, ref, link_sem.at[way, kind[1]], landed, device).start()

    def hand_over(kind, s, taps):
        ref = shards(kind, s, taps)
        remote(ref, ref, twin_s.at[kind[1]], twin_r.at[kind[1]], twin_id).start()

    def receive(kind, ref, landed):
        remote(ref, ref, link_sem.at[0, kind[1]], landed, twin_id).wait_recv()

    def far(kind):
        return DIRECT[kind[0] == "context"]

    def distance(j):
        return jnp.abs(others[j] - z)

    def z_send(kind, j):
        def act():
            device = (x, 2 * others[j] + y, c)
            send(kind, r, carried(kind), 0, z_sem.at[kind[1], z], device, own=True)

        if j < far(kind):
            act()
        else:
            pl.when(distance(j) <= far(kind))(act)

    def z_forward(kind, j):
        plane = others[j]
        beyond = z + jnp.where(plane < z, 1, -1)
        there = jnp.logical_and(beyond >= 0, beyond < planes)

        @pl.when(jnp.logical_and(there, distance(j) >= far(kind)))
        def _():
            device = (x, 2 * beyond + y, c)
            send(kind, 2 * plane + y, carried(kind), 0, z_sem.at[kind[1], plane], device)

    def whole_own(kind):
        return kind[0] == "cell"

    def y_taps(kind, j):
        return everything(kind) if whole_own(kind) and j < 0 else carried(kind)

    def relays(kind):
        return range(0 if whole_own(kind) else -1, reach)

    def own_send(kind, _):
        send(kind, r, y_taps(kind, -1), 1, y_sem.at[kind[1], z], beside, own=True)

    def z_step(kind, j):
        plane = others[j]
        s = 2 * plane + y
        receive(kind, shards(kind, s, carried(kind)), z_sem.at[kind[1], plane])
        if j + 1 >= far(kind) and far(kind) < reach:
            z_forward(kind, j)
        send(kind, s, carried(kind), 1, y_sem.at[kind[1], plane], beside)
        send(kind, s, only_here(kind), 2, x_sem.at[kind[1]], opposite)
        hand_over(kind, s, carried(kind))

    def y_step(kind, j):
        plane = z if j < 0 else others[j]
        s = 2 * plane + 1 - y
        receive(kind, shards(kind, s, y_taps(kind, j)), y_sem.at[kind[1], plane])
        if j in relays(kind):
            send(kind, s, only_here(kind), 1, relay_sem.at[kind[1]], opposite)
        hand_over(kind, s, y_taps(kind, j))

    def x_step(kind, _):
        taps = only_here(kind, True)
        receive(kind, several(kind, reach, taps), x_sem.at[kind[1]])
        for plane in others:
            hand_over(kind, 2 * plane + y, taps)

    def relay_step(kind, _):
        taps = only_here(kind, True)
        receive(kind, several(kind, len(relays(kind)), taps), relay_sem.at[kind[1]])
        for j in relays(kind):
            plane = z if j < 0 else others[j]
            hand_over(kind, 2 * plane + 1 - y, taps)

    def twin_waits(kind):
        ref = several(kind, n - 1, everything(kind))
        remote(ref, ref, twin_s.at[kind[1]], twin_r.at[kind[1]], twin_id).wait_recv()

    def sent_waits(kind):
        def sent(count, taps, sem):
            ref = several(kind, count, taps)
            remote(ref, ref, sem, twin_r.at[kind[1]], twin_id).wait_send()

        def sent_along_z(place):
            direct = sum(1 for p in range(planes) if 0 < abs(p - place) <= far(kind))
            passed = sum(
                1 for p in range(planes) for step in (-1, 1)
                if (place - p) * step >= far(kind) and 0 <= place + step < planes
            )
            sent(direct + passed, carried(kind), link_sem.at[0, kind[1]])

        if far(kind) >= reach:
            sent(reach, carried(kind), link_sem.at[0, kind[1]])
        else:
            for place in range(planes):
                pl.when(z == place)(functools.partial(sent_along_z, place))
        sent(planes, everything(kind), link_sem.at[1, kind[1]])
        sent(reach, only_here(kind), link_sem.at[2, kind[1]])
        sent(n - 1, everything(kind), twin_s.at[kind[1]])

    def plan_of(kinds, sends, times):
        plan = [(when, z_send, kind, j) for kind, when in zip(kinds, sends) for j in range(reach)]
        plan += [(when, own_send, kind, 0) for kind, when in zip(kinds, sends)]
        for kind, (start, pace, hop) in zip(kinds, times):
            plan.append((start + 0.5, y_step, kind, -1))
            for j in range(reach):
                there = start + pace * j
                plan.append((there, z_step, kind, j))
                plan.append((there + hop, y_step, kind, j))
            plan.append((there + hop - 0.1, x_step, kind, 0))
            plan.append((there + 2 * hop, relay_step, kind, 0))
        return sorted(plan, key=lambda entry: entry[0])

    spread = [CELL[0] + CELL[1] * a for a in range(len(cells))]
    cell_plan = plan_of(cells, [0.0] * len(cells), [(at,) + CELL[2:] for at in spread])
    context_plan = plan_of(contexts, SENDS, CONTEXTS)

    def take(plan, first, last):
        for when, step, kind, j in plan:
            if first <= when < last:
                step(kind, j)

    early = 0.1
    pl.when(odd_core)(lambda: take(cell_plan, 0.0, early))

    side = across + MARGIN
    rims = sum(pads)
    for d in (-1, 0, 1):
        there = row_inside(r + d) if d else None

        def rim(act, d=d):
            for t in range(steps):
                pad = pads[t]
                first, span, landing = {
                    -1: (0, pad, pad + height), 0: (0, height, pad), 1: (height - pad, pad, 0)
                }[d]
                for core in (c, twin):
                    if core is c and d == 0:
                        continue
                    if core is c:
                        left, extent, place = 0, across, MARGIN
                    else:
                        left = pl.multiple_of((1 - c) * (across - MARGIN), 16)
                        extent, place = MARGIN, pl.multiple_of(c * (across + MARGIN), 16)
                    act(
                        remote(
                            frames.at[x, t, pl.ds(first, span), pl.ds(left, extent)],
                            fp.at[t, pl.ds(landing, span), pl.ds(place, extent)],
                            ex_s.at[d + 1], ex_r.at[d + 1], (x, r + d, core),
                        )
                    )

        run(there, lambda: rim(lambda copy: copy.start()))

    def rim_ref(d):
        if d == 0:
            return fp.at[:, pl.ds(0, height), pl.ds(0, MARGIN)]
        return fp.at[0, pl.ds(0, rims), pl.ds(0, side)]

    def rims_arrive():
        for d in (-1, 0, 1):
            ref = rim_ref(d)
            copy = remote(ref, ref, ex_s.at[d + 1], ex_r.at[d + 1], twin_id)
            run(row_inside(r - d) if d else None, copy.wait_recv)

    def rims_leave():
        for d in (-1, 0, 1):
            ref = rim_ref(d)
            copy = remote(ref, ref, ex_s.at[d + 1], ex_r.at[d + 1], twin_id)
            run(row_inside(r + d) if d else None, copy.wait_send)

    for t in range(steps):
        pad = pads[t]
        total_rows = height + 2 * pad

        def blank(ref, first, count, left, extent):
            ref[first : first + count, left : left + extent] = jnp.zeros(
                (count, extent, ref.shape[-1]), ref.dtype
            )

        @pl.when(r == 0)
        def _(t=t, pad=pad):
            blank(fp.at[t], 0, pad, 0, across + 2 * MARGIN)

        @pl.when(r == n - 1)
        def _(t=t, pad=pad):
            blank(fp.at[t], pad + height, pad, 0, across + 2 * MARGIN)

        @pl.when(even_core)
        def _(t=t, total_rows=total_rows):
            blank(fp.at[t], 0, total_rows, 0, MARGIN)

        @pl.when(odd_core)
        def _(t=t, total_rows=total_rows):
            blank(fp.at[t], 0, total_rows, MARGIN + across, MARGIN)

    for ref, margin in ((f1, DILATIONS[0]), (f2, DILATIONS[1])):
        blank(ref, 0, ref.shape[0], 0, margin)
        blank(ref, 0, ref.shape[0], margin + 2 * across, margin)
    for ref, margin in [(hp.at[t], MARGIN) for t in range(steps - 1)]:
        @pl.when(even_core)
        def _(ref=ref, margin=margin):
            blank(ref, 0, ref.shape[0], 0, margin)

        @pl.when(odd_core)
        def _(ref=ref, margin=margin):
            blank(ref, 0, ref.shape[0], margin + across, margin)

    pl.when(odd_core)(lambda: take(cell_plan, early, 1e9))

    @pl.when(even_core)
    def _():
        take(context_plan, 0.0, PAUSE)
        for kind in cells:
            twin_waits(kind)

    local_wait(0, wc.at[:, r])
    local_wait(1, w1.at[r])
    local_wait(2, w23.at[:, r])
    local_wait(3, fp.at[:, pl.ds(0, height), pl.ds(0, across)])
    local_wait(4, biases)
    rims_arrive()

    cell_bias, first_bias, second_bias, third_bias = [
        biases[at : at + length].reshape(1, -1) for at, length in spans
    ]
    per = wc.shape[3]
    frame_sources = channels // per

    def tap_columns(buffer, count):
        taps = []
        for row in range(count):
            wide_row = buffer[row].astype(jnp.float32)
            length = wide_row.shape[0]
            taps.append(
                [
                    pltpu.roll(wide_row, 1, 0)[MARGIN : MARGIN + across].astype(jnp.bfloat16),
                    buffer[row, MARGIN : MARGIN + across],
                    pltpu.roll(wide_row, length - 1, 0)[MARGIN : MARGIN + across].astype(
                        jnp.bfloat16
                    ),
                ]
            )
        return taps

    def columns_of(buffer, count):
        taps = tap_columns(buffer, count + 2)
        return jnp.concatenate(
            [
                jnp.concatenate([taps[row + a][b] for row in range(count)], axis=0)
                for a in range(3)
                for b in range(3)
            ],
            axis=1,
        )

    def gate_part(left, sources):
        return [
            jnp.dot(
                left,
                jnp.concatenate([wc[half, s, t] for t in range(9) for s in sources], axis=0),
                preferred_element_type=jnp.float32,
            )
            for half in range(2)
        ]

    def update(gates, memory):
        inflow = jax.nn.sigmoid(gates[0][:, :state])
        output = jax.nn.sigmoid(gates[1][:, :state])
        fresh = inflow * jnp.tanh(gates[1][:, state:])
        if memory is None:
            memory = fresh
        else:
            memory = jax.nn.sigmoid(gates[0][:, state:]) * memory + fresh
        return (output * jnp.tanh(memory)).astype(jnp.bfloat16), memory

    swaps = []

    def exchange_columns(number, buffer, margin):
        sent = pl.multiple_of((1 - c) * across + c * margin, 16)
        landing = pl.multiple_of(c * (margin + across), 16)
        copy = pltpu.make_async_remote_copy(
            src_ref=buffer.at[:, pl.ds(sent, margin)],
            dst_ref=buffer.at[:, pl.ds(landing, margin)],
            send_sem=col_s.at[number],
            recv_sem=col_r.at[number],
            device_id=(x, r, twin),
            device_id_type=MESH_ID,
        )
        copy.start()
        departures.append(copy)
        return copy

    seen, unseen = range(frame_sources), range(frame_sources, n)
    counts = [height + 2 * (steps - 1 - t) for t in range(steps)]
    lefts = jnp.concatenate(
        [columns_of(fp.at[t], counts[t]) for t in range(steps)], axis=0
    )
    frame_gates = gate_part(lefts, seen)
    start = 0
    memory = None
    for t in range(steps):
        length = counts[t] * across
        gates = [
            part[start : start + length] + cell_bias[:, half * 2 * state : (half + 1) * 2 * state]
            for half, part in enumerate(frame_gates)
        ]
        start += length
        if t:
            swaps[-1].wait_recv()
            extra = gate_part(columns_of(hp.at[t - 1], counts[t]), unseen)
            gates = [one + more for one, more in zip(gates, extra)]
            memory = memory[across : memory.shape[0] - across]
        hidden, memory = update(gates, memory)
        if t == steps - 1:
            break
        view = hp.at[t]
        outside = steps - 1 - t
        for row in range(counts[t]):
            value = hidden[row * across : (row + 1) * across]
            if row < outside or row >= counts[t] - outside:
                place = r * height + row - outside
                valid = jnp.logical_and(place >= 0, place < n * height)
                value = jnp.where(valid, value, jnp.zeros_like(value))
            view[row, MARGIN : MARGIN + across] = value
        swaps.append(exchange_columns(t, view, MARGIN))


    def product(left, weight):
        return jnp.dot(
            left.reshape(-1, left.shape[-1]), weight, preferred_element_type=jnp.float32
        )

    margin = DILATIONS[0]
    block = pl.ds(pl.multiple_of(margin + c * across, 16), across)
    f1[:, block] = hidden.reshape(height, across, state)
    swap = pltpu.make_async_remote_copy(
        src_ref=f1.at[:, block], dst_ref=f1.at[:, block], send_sem=col_s.at[steps - 1],
        recv_sem=col_r.at[steps - 1], device_id=(x, r, twin), device_id_type=MESH_ID,
    )
    swap.start()
    departures.append(swap)

    @pl.when(even_core)
    def _():
        take(context_plan, PAUSE, 1e9)

    pl.when(odd_core)(lambda: twin_waits(contexts[0]))
    swap.wait_recv()

    def convolve(buffer, margin, weight, offset):
        total = None
        for b in range(3):
            more = product(buffer[:, b * margin : b * margin + 2 * across], weight(b))
            total = more if total is None else total + more
        return jnp.maximum(total + offset, 0.0).astype(jnp.bfloat16)

    first = convolve(
        f1, margin, lambda b: jnp.concatenate([w1[s, b] for s in range(n)], axis=0), first_bias
    )
    margin = DILATIONS[1]
    f2[:, margin : margin + 2 * across] = first.reshape(height, 2 * across, -1)
    rims_leave()

    @pl.when(odd_core)
    def _():
        for kind in cells:
            sent_waits(kind)
        twin_waits(contexts[1])

    second = convolve(
        f2, margin, lambda b: jnp.concatenate([w23[0, s, b] for s in range(n)], axis=0),
        second_bias,
    )
    second = second.reshape(height, 2, across, -1)
    for col in range(2):
        f3[col] = second[:, col]

    pl.when(odd_core)(lambda: twin_waits(contexts[2]))

    def last(b):
        return jnp.concatenate([w23[1, s, b] for s in range(n)], axis=0)

    feature = f3[c].reshape(height * across, -1)
    total = product(feature, last(1)) + product(f3[twin], last(2 - 2 * c))
    result = jnp.maximum(total + third_bias, 0.0)
    context = (feature.astype(jnp.float32) + result).astype(jnp.bfloat16)
    out[0] = context.reshape(out.shape[1:])

    @pl.when(even_core)
    def _():
        for kind in contexts:
            sent_waits(kind)

    for copy in departures:
        copy.wait_send()


def grid_device(n, *args):
    frames, cell_w, cell_b, first_w, first_b, second_w, second_b, third_w, third_b = args
    micro, steps, height, across, channels = frames.shape
    state, width = cell_b.shape[0] // 4, first_b.shape[0]
    depth = cell_w.shape[1]
    kinds = max(2 * (depth // 16 if depth % 16 == 0 else 1), 3)
    dma, bf16 = pltpu.SemaphoreType.DMA, jnp.bfloat16
    anywhere, vmem = pl.BlockSpec(memory_space=pl.ANY), pl.BlockSpec(memory_space=pltpu.VMEM)
    return pl.pallas_call(
        functools.partial(grid_kernel, n=n),
        out_shape=pltpu.VMEM((1, height, across, width), bf16),
        in_specs=[anywhere] * 9,
        out_specs=vmem,
        scratch_shapes=[
            pltpu.VMEM((2, n, 9, cell_w.shape[1], 2 * state), bf16),
            pltpu.VMEM((n, 3) + first_w.shape[1:], bf16),
            pltpu.VMEM((2, n, 3) + second_w.shape[1:], bf16),
            pltpu.VMEM((steps, height + 2 * steps, across + 2 * MARGIN, channels), bf16),
            pltpu.VMEM((steps - 1, height + 2 * (steps - 1), across + 2 * MARGIN, state), bf16),
            pltpu.VMEM((height, 2 * (across + DILATIONS[0]), state), bf16),
            pltpu.VMEM((height, 2 * (across + DILATIONS[1]), width), bf16),
            pltpu.VMEM((2, height, across, width), bf16),
            pltpu.VMEM((sum(v.shape[0] for v in (cell_b, first_b, second_b, third_b)),), jnp.float32),
            dma((5,)),
            dma((kinds, n // 2)),
            dma((kinds, n // 2)),
            dma((kinds,)),
            dma((kinds,)),
            dma((3, kinds)),
            dma((kinds,)),
            dma((kinds,)),
            dma((3,)),
            dma((3,)),
            dma((steps,)),
            dma((steps,)),
        ],
        compiler_params=pltpu.CompilerParams(collective_id=1, has_side_effects=True),
    )(*args)


def fits_grid(mesh, frames):
    n, cols = mesh.shape["rows"], mesh.shape["cols"]
    micro, steps, height, across, channels = frames.shape
    return (
        mesh.shape["segment"] == 2 and cols == 2 and n % 2 == 0 and n > 2
        and min(DILATIONS) // height >= n and DILATIONS[-1] == across
        and max(DILATIONS[:-1]) <= across and steps <= height
    )


def solution(mesh):
    kernels = P(None, "rows", None)
    placed = (
        P(None, None, "rows", "cols", None),
        kernels, P(), kernels, P(), kernels, P(), kernels, P(),
    )
    n, cols = mesh.shape["rows"], mesh.shape["cols"]

    def on_device(*args):
        if fits_grid(mesh, args[0]):
            return grid_device(n, *args)
        return per_device(n, cols, mesh.shape["segment"] == 2, *args)

    return jax.shard_map(
        on_device,
        mesh=mesh,
        in_specs=placed,
        out_specs=P("segment", "rows", "cols", None),
        check_vma=False,
    )
```

```python
import functools

import jax
import jax.numpy as jnp
from jax import lax
from jax.experimental import pallas as pl
from jax.experimental.pallas import tpu as pltpu
from jax.sharding import PartitionSpec as P

DILATIONS = (16, 32, 64)
MESH_ID = pl.DeviceIdType.MESH
MARGIN = 16
CELL = (3.2, 1.3, 1.0, 2.8)
SENDS = (0.2, 0.3, 0.4)
CONTEXTS = ((4.0, 1.0, 3.2), (7.0, 1.0, 3.2), (9.0, 1.0, 3.2))
PAUSE = 17.0
DIRECT = (99, 2)


def encoder_kernel(
    frames, cell_w, cell_b, first_w, first_b, second_w, second_b, third_w, third_b,
    out, wc, w1, w2, w3, fp, hp, f1, f2, f3,
    local_sem, ring_s, ring_r, across_s, across_r, pair_s, pair_r, ex_s, ex_r, *, n, cols, shared, row_pads,
):
    seg, r, c = lax.axis_index("segment"), lax.axis_index("rows"), lax.axis_index("cols")
    steps, height, across, channels = frames.shape[1:]
    state = cell_b.shape[-1] // 4
    half = n // 2
    odd = lax.rem(c, 2)
    even_core, odd_core = odd == 0, odd == 1
    sign = 1 - 2 * odd
    parity, pair = lax.rem(r, 2), lax.div(r, 2)
    place = pair + parity * (n - 1 - 2 * pair)

    def rows_at(position):
        upper = lax.div(position, half)
        return 2 * position + upper * (2 * n - 1 - 4 * position)

    behind_rows = [r] + [rows_at(lax.rem(place - sign * k + n, n)) for k in range(1, half + 1)]
    ahead_rows = [r] + [rows_at(lax.rem(place + sign * k + n, n)) for k in range(1, half + 1)]
    following, preceding = ahead_rows[1], behind_rows[1]
    partner = c + 1 - 2 * odd
    ahead_id, partner_id = (seg, following, c), (seg, r, partner)

    reaches = sorted({1} | {s // height for s, pad in zip(DILATIONS, row_pads) if pad})
    offsets = [(0, -1), (0, 1)] + [
        (d * reach, dc) for reach in reaches for d in (-1, 1) for dc in (-1, 0, 1)
    ]

    def present(dr, dc):
        row, col = r + dr, c + dc
        return jnp.logical_and(
            jnp.logical_and(row >= 0, row < n), jnp.logical_and(col >= 0, col < cols)
        )

    inside = {offset: present(*offset) for offset in offsets}

    locals_ = []
    for t in range(steps):
        locals_.append(
            pltpu.make_async_copy(
                frames.at[seg, t],
                fp.at[t, pl.ds(1, height), pl.ds(MARGIN, across)],
                local_sem.at[t],
            )
        )
    stored = (cell_w, first_w, second_w, third_w)
    gathered = (wc, w1, w2, w3)
    own = []
    for ref, whole in zip(stored, gathered):
        taps = whole.shape[1]
        own.append(ref.at[pl.ds((9 - taps) // 2, taps)])
    for a in range(4):
        locals_.append(
            pltpu.make_async_copy(own[a], gathered[a].at[r], local_sem.at[steps + a])
        )
    for t in range(steps):
        fp[t] = jnp.zeros(fp.shape[1:], fp.dtype)
    for t in range(hp.shape[0]):
        hp[t] = jnp.zeros(hp.shape[1:], hp.dtype)
    for buffer in (f1, f2, f3):
        buffer[...] = jnp.zeros(buffer.shape, buffer.dtype)
    for copy in locals_:
        copy.start()

    barrier = pltpu.get_barrier_semaphore()
    expected = jnp.int32(2)
    for target in (following, preceding):
        pl.semaphore_signal(barrier, inc=1, device_id=(seg, target, c), device_id_type=MESH_ID)
    for dr, dc in offsets:
        there = inside[dr, dc]
        expected = expected + there.astype(jnp.int32)

        @pl.when(there)
        def _():
            pl.semaphore_signal(
                barrier, inc=1, device_id=(seg, r + dr, c + dc), device_id_type=MESH_ID
            )

    if shared:
        expected = expected + 1
        pl.semaphore_signal(barrier, inc=1, device_id=(1 - seg, r, c), device_id_type=MESH_ID)
    pl.semaphore_wait(barrier, expected)

    def exchange(number, source_of, buffer, pad, reach, width):
        arrivals, departures = [], []
        for i, (dr, dc) in enumerate((a, b) for a in (-1, 0, 1) for b in (-1, 0, 1)):
            if (dr, dc) == (0, 0) or (dr and not pad):
                continue
            first, span, landing = {
                -1: (0, pad, pad + height), 0: (0, height, pad), 1: (height - pad, pad, 0)
            }[dr]
            left, extent, side = {
                -1: (0, width[1], width[0] + across),
                0: (0, across, width[0]),
                1: (across - width[1], width[1], width[0] - width[1]),
            }[dc]
            copy = pltpu.make_async_remote_copy(
                src_ref=source_of(first, span, left, extent),
                dst_ref=buffer.at[pl.ds(landing, span), pl.ds(side, extent)],
                send_sem=ex_s.at[number, i],
                recv_sem=ex_r.at[number, i],
                device_id=(seg, r + dr * reach, c + dc),
                device_id_type=MESH_ID,
            )
            there, behind = inside[dr * reach, dc], inside[-dr * reach, -dc]
            pl.when(there)(copy.start)
            departures.append((there, copy))
            arrivals.append((behind, copy))

        def arrive():
            for behind, copy in arrivals:
                pl.when(behind)(copy.wait_recv)

        def depart():
            for there, copy in departures:
                pl.when(there)(copy.wait_send)

        return arrive, depart

    def block_of(buffer, pad, margin):
        return lambda first, span, left, extent: buffer.at[
            pl.ds(pad + first, span), pl.ds(margin + left, extent)
        ]

    departs = []
    frame_arrivals = []
    for t in range(steps):
        arrive, depart = exchange(
            t,
            lambda first, span, left, extent, t=t: frames.at[
                seg, t, pl.ds(first, span), pl.ds(left, extent)
            ],
            fp.at[t], 1, 1, (MARGIN, MARGIN),
        )
        frame_arrivals.append(arrive)
        departs.append(depart)

    parts = (2 * seg, 1, 2 * (1 - seg)) if shared else (0, 1, 2)
    carried = range(2) if shared else range(3)

    def slot(a, part, k):
        span = gathered[a].shape[1] // 3
        source = behind_rows[k] if k >= 0 else ahead_rows[-k]
        return gathered[a].at[source, pl.ds(parts[part] * span, span)]

    def ring_copy(a, part, k, sent=True):
        span = gathered[a].shape[1] // 3
        place_of = slot(a, part, k if sent else k + 1)
        start = (9 - 3 * span) // 2 + parts[part] * span
        return pltpu.make_async_remote_copy(
            src_ref=stored[a].at[pl.ds(start, span)] if sent and k == 0 else place_of,
            dst_ref=place_of,
            send_sem=ring_s.at[a, part, k],
            recv_sem=ring_r.at[a, part, k],
            device_id=ahead_id,
            device_id_type=MESH_ID,
        )

    def across_copy(a, k, sent=True):
        piece = slot(a, 0 if sent else 2, k)
        return pltpu.make_async_remote_copy(
            src_ref=piece, dst_ref=piece, send_sem=across_s.at[a, k], recv_sem=across_r.at[a, k],
            device_id=(1 - seg, r, c), device_id_type=MESH_ID,
        )

    def pair_copy(a, part, k, direction):
        piece = slot(a, part, direction * k)
        return pltpu.make_async_remote_copy(
            src_ref=piece, dst_ref=piece, send_sem=pair_s.at[a, part, k],
            recv_sem=pair_r.at[a, part, k], device_id=partner_id, device_id_type=MESH_ID,
        )

    def longer(a):
        return even_core if a == 0 else odd_core

    def guarded(condition, act):
        if condition is None:
            act()
        else:
            pl.when(condition)(act)

    def ring_send(a, part, k):
        guarded(longer(a) if k == half - 1 else None, ring_copy(a, part, k).start)

    def own_send(a):
        for part in carried:
            ring_send(a, part, 0)

    def ring_step(a, k):
        def act():
            for part in carried:
                ring_copy(a, part, k - 1, False).wait_recv()
                if k < half:
                    ring_send(a, part, k)
                if shared and part == 0:
                    across_copy(a, k).start()
                pair_copy(a, part, k, 1).start()

        guarded(longer(a) if k == half else None, act)

    def across_step(a, k):
        def act():
            across_copy(a, k, False).wait_recv()
            pair_copy(a, 2, k, 1).start()

        if shared:
            guarded(longer(a) if k == half else None, act)

    def pair_waits(a):
        shorter = odd_core if a == 0 else even_core
        for k in range(1, half + 1):
            for part in range(3):
                guarded(
                    shorter if k == half else None, pair_copy(a, part, k, -1).wait_recv
                )

    context_steps = list(range(1, half + 1))
    quarter = max(1, half // 4)

    def context_ring(count):
        for _ in range(min(count, len(context_steps))):
            k = context_steps.pop(0)
            for a in (1, 2, 3):
                ring_step(a, k)
            if k > 1:
                for a in (1, 2, 3):
                    across_step(a, k - 1)

    own_send(0)
    for k in range(1, half + 1):
        ring_step(0, k)
        if k > 1:
            across_step(0, k - 1)
        if k == 1:
            for a in (1, 2, 3):
                own_send(a)
        else:
            context_ring(1)
    context_ring(quarter)
    across_step(0, half)

    for copy in locals_:
        copy.wait()
    for arrive in frame_arrivals:
        arrive()
    pair_waits(0)

    bias = cell_b[...].reshape(1, -1)
    per = wc.shape[2]
    frame_sources = channels // per

    def tap_columns(buffer):
        taps = []
        for row in range(height + 2):
            wide = buffer[row].astype(jnp.float32)
            length = wide.shape[0]
            taps.append(
                [
                    pltpu.roll(wide, 1, 0)[MARGIN : MARGIN + across].astype(jnp.bfloat16),
                    buffer[row, MARGIN : MARGIN + across],
                    pltpu.roll(wide, length - 1, 0)[MARGIN : MARGIN + across].astype(
                        jnp.bfloat16
                    ),
                ]
            )
        return taps

    def gate_part(buffer, sources):
        taps = tap_columns(buffer)
        left = jnp.concatenate(
            [
                jnp.concatenate([taps[row + a][b] for row in range(height)], axis=0)
                for a in range(3)
                for b in range(3)
            ],
            axis=1,
        )
        right = jnp.concatenate([wc[s, t] for t in range(9) for s in sources], axis=0)
        return jnp.dot(left, right, preferred_element_type=jnp.float32)

    def update(gates, memory):
        inflow = jax.nn.sigmoid(gates[:, :state])
        forget = jax.nn.sigmoid(gates[:, state : 2 * state])
        output = jax.nn.sigmoid(gates[:, 2 * state : 3 * state])
        fresh = inflow * jnp.tanh(gates[:, 3 * state :])
        memory = fresh if memory is None else forget * memory + fresh
        return (output * jnp.tanh(memory)).astype(jnp.bfloat16), memory

    seen, unseen = range(frame_sources), range(frame_sources, n)
    hidden, memory = update(gate_part(fp.at[0], seen) + bias, None)
    for t in range(1, steps):
        view = hp.at[t - 1]
        for row in range(height):
            view[1 + row, MARGIN : MARGIN + across] = hidden[row * across : (row + 1) * across]
        arrive, depart = exchange(
            steps + t - 1, block_of(view, 1, MARGIN), view, 1, 1, (MARGIN, MARGIN)
        )
        departs.append(depart)
        context_ring(quarter)
        gates = gate_part(fp.at[t], seen) + bias
        context_ring(quarter)
        arrive()
        hidden, memory = update(gates + gate_part(view, unseen), memory)

    feature = hidden
    layers = ((f1, w1, first_b), (f2, w2, second_b), (f3, w3, third_b))
    for i, (buffer, weight, offset) in enumerate(layers):
        spacing, pad = DILATIONS[i], row_pads[i]
        for row in range(height):
            buffer[pad + row, spacing : spacing + across] = feature[
                row * across : (row + 1) * across
            ]
        arrive, depart = exchange(
            2 * steps - 1 + i, block_of(buffer, pad, spacing), buffer, pad,
            spacing // height, (spacing, spacing),
        )
        departs.append(depart)
        if i == 0:
            context_ring(len(context_steps))
            for a in (1, 2, 3):
                across_step(a, half)
        pair_waits(i + 1)
        arrive()
        total = None
        taps = weight.shape[1]
        for t in range(taps):
            a, b = t // 3, t % 3
            left = buffer[a * pad : a * pad + height, b * spacing : b * spacing + across]
            left = left.reshape(height * across, left.shape[-1])
            right = jnp.concatenate([weight[s, t] for s in range(n)], axis=0)
            product = jnp.dot(left, right, preferred_element_type=jnp.float32)
            total = product if total is None else total + product
        result = jnp.maximum(total + offset[...].reshape(1, -1), 0.0)
        if i < 2:
            feature = result.astype(jnp.bfloat16)
    context = (feature.astype(jnp.float32) + result).astype(jnp.bfloat16)
    out[0] = context.reshape(out.shape[1:])

    for depart in departs:
        depart()
    for a in range(4):
        for k in range(half):
            for part in carried:
                guarded(
                    longer(a) if k == half - 1 else None, ring_copy(a, part, k).wait_send
                )
        for k in range(1, half + 1):
            for part in range(3):
                guarded(longer(a) if k == half else None, pair_copy(a, part, k, 1).wait_send)
            if shared:
                guarded(longer(a) if k == half else None, across_copy(a, k).wait_send)


def per_device(n, cols, shared, *args):
    frames, cell_w, cell_b, first_w, first_b, second_w, second_b, third_w, third_b = args
    micro, steps, height, across, channels = frames.shape
    state, width = cell_b.shape[0] // 4, first_b.shape[0]
    row_pads = tuple(height if s // height < n else 0 for s in DILATIONS)

    def slots(weight, pad):
        return pltpu.VMEM((n, 9 if pad else 3) + weight.shape[1:], weight.dtype)

    def field(spacing, pad, depth):
        return pltpu.VMEM((height + 2 * pad, across + 2 * spacing, depth), jnp.bfloat16)

    half = n // 2
    exchanges = 2 * steps - 1 + 3
    dma = pltpu.SemaphoreType.DMA
    anywhere, vmem = pl.BlockSpec(memory_space=pl.ANY), pl.BlockSpec(memory_space=pltpu.VMEM)
    return pl.pallas_call(
        functools.partial(encoder_kernel, n=n, cols=cols, shared=shared, row_pads=row_pads),
        out_shape=jax.ShapeDtypeStruct((1, height, across, width), jnp.bfloat16),
        in_specs=[anywhere, anywhere, vmem, anywhere, vmem, anywhere, vmem, anywhere, vmem],
        out_specs=vmem,
        scratch_shapes=[
            slots(cell_w, 1),
            slots(first_w, row_pads[0]),
            slots(second_w, row_pads[1]),
            slots(third_w, row_pads[2]),
            pltpu.VMEM((steps, height + 2, across + 2 * MARGIN, channels), jnp.bfloat16),
            pltpu.VMEM((steps - 1, height + 2, across + 2 * MARGIN, state), jnp.bfloat16),
            field(DILATIONS[0], row_pads[0], state),
            field(DILATIONS[1], row_pads[1], width),
            field(DILATIONS[2], row_pads[2], width),
            dma((steps + 4,)),
            dma((4, 3, half)),
            dma((4, 3, half)),
            dma((4, half + 1)),
            dma((4, half + 1)),
            dma((4, 3, half + 1)),
            dma((4, 3, half + 1)),
            dma((exchanges, 9)),
            dma((exchanges, 9)),
        ],
        compiler_params=pltpu.CompilerParams(collective_id=0, has_side_effects=True),
    )(
        frames, cell_w, cell_b, first_w, first_b, second_w, second_b,
        third_w, third_b,
    )


def grid_kernel(
    frames, cell_w, cell_b, first_w, first_b, second_w, second_b, third_w, third_b,
    out, wc, w1, w23, fp, hp, f1, f2, f3, biases,
    local_sem, z_sem, y_sem, x_sem, relay_sem, link_sem, twin_s, twin_r, ex_s, ex_r, col_s, col_r,
    *, n,
):
    x, r, c = lax.axis_index("segment"), lax.axis_index("rows"), lax.axis_index("cols")
    steps, height, across, channels = frames.shape[1:]
    state = cell_b.shape[-1] // 4
    planes = n // 2
    reach = planes - 1
    z, y = lax.div(r, 2), lax.rem(r, 2)
    ry = r + 1 - 2 * y
    twin = 1 - c
    even_core, odd_core = c == 0, c == 1

    def run(condition, act):
        if condition is None:
            act()
        else:
            pl.when(condition)(act)

    near_side = jnp.where(z < planes - 1 - z, z, planes - 1 - z)
    long_side = jnp.where(z < planes - 1 - z, 1, -1)

    def other(j):
        paired = j < 2 * near_side
        k = jnp.where(paired, j // 2 + 1, j + 1 - near_side)
        return z + jnp.where(paired, long_side * (1 - 2 * (j % 2)), long_side) * k

    others = [other(j) for j in range(reach)]

    pads = [steps - t for t in range(steps)]
    locals_ = [
        pltpu.make_async_copy(
            cell_w.at[:, :, pl.ds(half * 2 * state, 2 * state)], wc.at[half, r],
            local_sem.at[0],
        )
        for half in range(2)
    ]
    locals_.append(pltpu.make_async_copy(first_w.at[pl.ds(3, 3)], w1.at[r], local_sem.at[1]))
    for half, weight in enumerate((second_w, third_w)):
        locals_.append(
            pltpu.make_async_copy(weight.at[pl.ds(3, 3)], w23.at[half, r], local_sem.at[2])
        )
    for t in range(steps):
        locals_.append(
            pltpu.make_async_copy(
                frames.at[x, t],
                fp.at[t, pl.ds(pads[t], height), pl.ds(MARGIN, across)],
                local_sem.at[3],
            )
        )
    offset = 0
    spans = []
    for vector in (cell_b, first_b, second_b, third_b):
        length = vector.shape[0]
        spans.append((offset, length))
        locals_.append(
            pltpu.make_async_copy(vector, biases.at[pl.ds(offset, length)], local_sem.at[4])
        )
        offset += length
    for copy in locals_:
        copy.start()

    def local_wait(number, ref):
        pltpu.make_async_copy(ref, ref, local_sem.at[number]).wait()

    def row_inside(row):
        return jnp.logical_and(row >= 0, row < n)

    barrier = pltpu.get_barrier_semaphore()
    expected = jnp.int32(2 + reach)
    pl.semaphore_signal(barrier, inc=1, device_id=(1 - x, r, c), device_id_type=MESH_ID)
    pl.semaphore_signal(barrier, inc=1, device_id=(x, r, twin), device_id_type=MESH_ID)
    for plane in others:
        pl.semaphore_signal(
            barrier, inc=1, device_id=(x, 2 * plane + y, c), device_id_type=MESH_ID
        )
    for d in (-1, 1):
        there = row_inside(r + d)
        expected = expected + 2 * there.astype(jnp.int32)

        @pl.when(there)
        def _(d=d):
            for core in (c, twin):
                pl.semaphore_signal(
                    barrier, inc=1, device_id=(x, r + d, core), device_id_type=MESH_ID
                )

    pl.semaphore_wait(barrier, expected)

    depth = wc.shape[3]
    part_rows = 16 if depth % 16 == 0 else depth
    parts = [
        (half, pl.ds(first, part_rows)) for half in range(2) for first in range(0, depth, part_rows)
    ]
    cells = [("cell", a) for a in range(len(parts))]
    contexts = [("context", a) for a in range(3)]

    def taps_of(kind):
        return wc.shape[2] if kind[0] == "cell" else w1.shape[1]

    def complete(kind):
        return kind == ("context", 0)

    def carried(kind):
        if complete(kind):
            return everything(kind)
        larger = (taps_of(kind) + 1) // 2
        return (taps_of(kind) - larger) * x, larger

    def only_here(kind, there=False):
        larger = (taps_of(kind) + 1) // 2
        return larger * (1 - x if there else x), taps_of(kind) - larger

    def everything(kind):
        return 0, taps_of(kind)

    def shards(kind, s, taps):
        taps = pl.ds(*taps)
        if kind[0] == "cell":
            half, rows = parts[kind[1]]
            return wc.at[half, s, taps, rows]
        if kind[1] == 0:
            return w1.at[s, taps]
        return w23.at[kind[1] - 1, s, taps]

    def several(kind, count, taps):
        return shards(kind, pl.ds(0, count), taps)

    def stored(kind, taps):
        if kind[0] == "cell":
            half, rows = parts[kind[1]]
            return cell_w.at[pl.ds(*taps), rows, pl.ds(half * 2 * state, 2 * state)]
        whole = (first_w, second_w, third_w)[kind[1]]
        return whole.at[pl.ds((whole.shape[0] - taps_of(kind)) // 2 + taps[0], taps[1])]

    twin_id, beside, opposite = (x, r, twin), (x, ry, c), (1 - x, r, c)
    departures = []

    def remote(source, ref, sent, landed, device):
        return pltpu.make_async_remote_copy(
            src_ref=source, dst_ref=ref, send_sem=sent, recv_sem=landed,
            device_id=device, device_id_type=MESH_ID,
        )

    def send(kind, s, taps, way, landed, device, own=False):
        ref = shards(kind, s, taps)
        source = stored(kind, taps) if own else ref
        remote(source, ref, link_sem.at[way, kind[1]], landed, device).start()

    def hand_over(kind, s, taps):
        ref = shards(kind, s, taps)
        remote(ref, ref, twin_s.at[kind[1]], twin_r.at[kind[1]], twin_id).start()

    def receive(kind, ref, landed):
        remote(ref, ref, link_sem.at[0, kind[1]], landed, twin_id).wait_recv()

    def far(kind):
        return DIRECT[kind[0] == "context"]

    def distance(j):
        return jnp.abs(others[j] - z)

    def z_send(kind, j):
        def act():
            device = (x, 2 * others[j] + y, c)
            send(kind, r, carried(kind), 0, z_sem.at[kind[1], z], device, own=True)

        if j < far(kind):
            act()
        else:
            pl.when(distance(j) <= far(kind))(act)

    def z_forward(kind, j):
        plane = others[j]
        beyond = z + jnp.where(plane < z, 1, -1)
        there = jnp.logical_and(beyond >= 0, beyond < planes)

        @pl.when(jnp.logical_and(there, distance(j) >= far(kind)))
        def _():
            device = (x, 2 * beyond + y, c)
            send(kind, 2 * plane + y, carried(kind), 0, z_sem.at[kind[1], plane], device)

    def whole_own(kind):
        return True

    def y_taps(kind, j):
        return everything(kind) if whole_own(kind) and j < 0 else carried(kind)

    def relays(kind):
        return range(reach if complete(kind) else 0, reach)

    def own_send(kind, _):
        send(kind, r, y_taps(kind, -1), 1, y_sem.at[kind[1], z], beside, own=True)

    def z_step(kind, j):
        plane = others[j]
        s = 2 * plane + y
        receive(kind, shards(kind, s, carried(kind)), z_sem.at[kind[1], plane])
        if j + 1 >= far(kind) and far(kind) < reach:
            z_forward(kind, j)
        send(kind, s, carried(kind), 1, y_sem.at[kind[1], plane], beside)
        if not complete(kind):
            send(kind, s, only_here(kind), 2, x_sem.at[kind[1]], opposite)
        if complete(kind):
            hand_over(kind, s, carried(kind))

    def y_step(kind, j):
        plane = z if j < 0 else others[j]
        s = 2 * plane + 1 - y
        receive(kind, shards(kind, s, y_taps(kind, j)), y_sem.at[kind[1], plane])
        if j in relays(kind):
            send(kind, s, only_here(kind), 1, relay_sem.at[kind[1]], opposite)
        hand_over(kind, s, y_taps(kind, j))

    def x_step(kind, _):
        taps = only_here(kind, True)
        receive(kind, several(kind, reach, taps), x_sem.at[kind[1]])
        for plane in others:
            hand_over(kind, 2 * plane + y, everything(kind))

    def relay_step(kind, _):
        taps = only_here(kind, True)
        receive(kind, several(kind, len(relays(kind)), taps), relay_sem.at[kind[1]])
        for j in relays(kind):
            plane = z if j < 0 else others[j]
            hand_over(kind, 2 * plane + 1 - y, taps)

    def twin_waits(kind):
        ref = several(kind, n - 1, everything(kind))
        remote(ref, ref, twin_s.at[kind[1]], twin_r.at[kind[1]], twin_id).wait_recv()

    def sent_waits(kind):
        def sent(count, taps, sem):
            ref = several(kind, count, taps)
            remote(ref, ref, sem, twin_r.at[kind[1]], twin_id).wait_send()

        def sent_along_z(place):
            direct = sum(1 for p in range(planes) if 0 < abs(p - place) <= far(kind))
            passed = sum(
                1 for p in range(planes) for step in (-1, 1)
                if (place - p) * step >= far(kind) and 0 <= place + step < planes
            )
            sent(direct + passed, carried(kind), link_sem.at[0, kind[1]])

        if far(kind) >= reach:
            sent(reach, carried(kind), link_sem.at[0, kind[1]])
        else:
            for place in range(planes):
                pl.when(z == place)(functools.partial(sent_along_z, place))
        sent(planes, everything(kind), link_sem.at[1, kind[1]])
        if not complete(kind):
            sent(reach, only_here(kind), link_sem.at[2, kind[1]])
        sent(n - 1, everything(kind), twin_s.at[kind[1]])

    def plan_of(kinds, sends, times):
        plan = [(when, z_send, kind, j) for kind, when in zip(kinds, sends) for j in range(reach)]
        plan += [(when, own_send, kind, 0) for kind, when in zip(kinds, sends)]
        for kind, (start, pace, hop) in zip(kinds, times):
            plan.append((start + 0.5, y_step, kind, -1))
            for j in range(reach):
                there = start + pace * j
                plan.append((there, z_step, kind, j))
                plan.append((there + hop, y_step, kind, j))
            if not complete(kind):
                plan.append((there + hop - 0.1, x_step, kind, 0))
                plan.append((there + 2 * hop, relay_step, kind, 0))
        return sorted(plan, key=lambda entry: entry[0])

    spread = [CELL[0] + CELL[1] * a for a in range(len(cells))]
    cell_plan = plan_of(cells, [0.0] * len(cells), [(at,) + CELL[2:] for at in spread])
    context_plan = plan_of(contexts, SENDS, CONTEXTS)

    def take(plan, first, last):
        for when, step, kind, j in plan:
            if first <= when < last:
                step(kind, j)

    early = 0.1
    pl.when(odd_core)(lambda: take(cell_plan, 0.0, early))

    side = across + MARGIN
    rims = sum(pads)
    for d in (-1, 0, 1):
        there = row_inside(r + d) if d else None

        def rim(act, d=d):
            for t in range(steps):
                pad = pads[t]
                first, span, landing = {
                    -1: (0, pad, pad + height), 0: (0, height, pad), 1: (height - pad, pad, 0)
                }[d]
                for core in (c, twin):
                    if core is c and d == 0:
                        continue
                    if core is c:
                        left, extent, place = 0, across, MARGIN
                    else:
                        left = pl.multiple_of((1 - c) * (across - MARGIN), 16)
                        extent, place = MARGIN, pl.multiple_of(c * (across + MARGIN), 16)
                    act(
                        remote(
                            frames.at[x, t, pl.ds(first, span), pl.ds(left, extent)],
                            fp.at[t, pl.ds(landing, span), pl.ds(place, extent)],
                            ex_s.at[d + 1], ex_r.at[d + 1], (x, r + d, core),
                        )
                    )

        run(there, lambda: rim(lambda copy: copy.start()))

    def rim_ref(d):
        if d == 0:
            return fp.at[:, pl.ds(0, height), pl.ds(0, MARGIN)]
        return fp.at[0, pl.ds(0, rims), pl.ds(0, side)]

    def rims_arrive():
        for d in (-1, 0, 1):
            ref = rim_ref(d)
            copy = remote(ref, ref, ex_s.at[d + 1], ex_r.at[d + 1], twin_id)
            run(row_inside(r - d) if d else None, copy.wait_recv)

    def rims_leave():
        for d in (-1, 0, 1):
            ref = rim_ref(d)
            copy = remote(ref, ref, ex_s.at[d + 1], ex_r.at[d + 1], twin_id)
            run(row_inside(r + d) if d else None, copy.wait_send)

    for t in range(steps):
        pad = pads[t]
        total_rows = height + 2 * pad

        def blank(ref, first, count, left, extent):
            ref[first : first + count, left : left + extent] = jnp.zeros(
                (count, extent, ref.shape[-1]), ref.dtype
            )

        @pl.when(r == 0)
        def _(t=t, pad=pad):
            blank(fp.at[t], 0, pad, 0, across + 2 * MARGIN)

        @pl.when(r == n - 1)
        def _(t=t, pad=pad):
            blank(fp.at[t], pad + height, pad, 0, across + 2 * MARGIN)

        @pl.when(even_core)
        def _(t=t, total_rows=total_rows):
            blank(fp.at[t], 0, total_rows, 0, MARGIN)

        @pl.when(odd_core)
        def _(t=t, total_rows=total_rows):
            blank(fp.at[t], 0, total_rows, MARGIN + across, MARGIN)

    for ref, margin in ((f1, DILATIONS[0]), (f2, DILATIONS[1])):
        blank(ref, 0, ref.shape[0], 0, margin)
        blank(ref, 0, ref.shape[0], margin + 2 * across, margin)
    for ref, margin in [(hp.at[t], MARGIN) for t in range(steps - 1)]:
        @pl.when(even_core)
        def _(ref=ref, margin=margin):
            blank(ref, 0, ref.shape[0], 0, margin)

        @pl.when(odd_core)
        def _(ref=ref, margin=margin):
            blank(ref, 0, ref.shape[0], margin + across, margin)

    pl.when(odd_core)(lambda: take(cell_plan, early, 1e9))

    @pl.when(even_core)
    def _():
        take(context_plan, 0.0, PAUSE)
        for kind in cells:
            twin_waits(kind)

    local_wait(0, wc.at[:, r])
    local_wait(1, w1.at[r])
    local_wait(2, w23.at[:, r])
    local_wait(3, fp.at[:, pl.ds(0, height), pl.ds(0, across)])
    local_wait(4, biases)
    rims_arrive()

    cell_bias, first_bias, second_bias, third_bias = [
        biases[at : at + length].reshape(1, -1) for at, length in spans
    ]
    per = wc.shape[3]
    frame_sources = channels // per

    def tap_columns(buffer, count):
        taps = []
        for row in range(count):
            wide_row = buffer[row].astype(jnp.float32)
            length = wide_row.shape[0]
            taps.append(
                [
                    pltpu.roll(wide_row, 1, 0)[MARGIN : MARGIN + across].astype(jnp.bfloat16),
                    buffer[row, MARGIN : MARGIN + across],
                    pltpu.roll(wide_row, length - 1, 0)[MARGIN : MARGIN + across].astype(
                        jnp.bfloat16
                    ),
                ]
            )
        return taps

    def columns_of(buffer, count):
        taps = tap_columns(buffer, count + 2)
        return jnp.concatenate(
            [
                jnp.concatenate([taps[row + a][b] for row in range(count)], axis=0)
                for a in range(3)
                for b in range(3)
            ],
            axis=1,
        )

    def gate_part(left, sources):
        return [
            jnp.dot(
                left,
                jnp.concatenate([wc[half, s, t] for t in range(9) for s in sources], axis=0),
                preferred_element_type=jnp.float32,
            )
            for half in range(2)
        ]

    def update(gates, memory):
        inflow = jax.nn.sigmoid(gates[0][:, :state])
        output = jax.nn.sigmoid(gates[1][:, :state])
        fresh = inflow * jnp.tanh(gates[1][:, state:])
        if memory is None:
            memory = fresh
        else:
            memory = jax.nn.sigmoid(gates[0][:, state:]) * memory + fresh
        return (output * jnp.tanh(memory)).astype(jnp.bfloat16), memory

    swaps = []

    def exchange_columns(number, buffer, margin):
        sent = pl.multiple_of((1 - c) * across + c * margin, 16)
        landing = pl.multiple_of(c * (margin + across), 16)
        copy = pltpu.make_async_remote_copy(
            src_ref=buffer.at[:, pl.ds(sent, margin)],
            dst_ref=buffer.at[:, pl.ds(landing, margin)],
            send_sem=col_s.at[number],
            recv_sem=col_r.at[number],
            device_id=(x, r, twin),
            device_id_type=MESH_ID,
        )
        copy.start()
        departures.append(copy)
        return copy

    seen, unseen = range(frame_sources), range(frame_sources, n)
    counts = [height + 2 * (steps - 1 - t) for t in range(steps)]
    lefts = jnp.concatenate(
        [columns_of(fp.at[t], counts[t]) for t in range(steps)], axis=0
    )
    frame_gates = gate_part(lefts, seen)
    start = 0
    memory = None
    for t in range(steps):
        length = counts[t] * across
        gates = [
            part[start : start + length] + cell_bias[:, half * 2 * state : (half + 1) * 2 * state]
            for half, part in enumerate(frame_gates)
        ]
        start += length
        if t:
            swaps[-1].wait_recv()
            extra = gate_part(columns_of(hp.at[t - 1], counts[t]), unseen)
            gates = [one + more for one, more in zip(gates, extra)]
            memory = memory[across : memory.shape[0] - across]
        hidden, memory = update(gates, memory)
        if t == steps - 1:
            break
        view = hp.at[t]
        outside = steps - 1 - t
        for row in range(counts[t]):
            value = hidden[row * across : (row + 1) * across]
            if row < outside or row >= counts[t] - outside:
                place = r * height + row - outside
                valid = jnp.logical_and(place >= 0, place < n * height)
                value = jnp.where(valid, value, jnp.zeros_like(value))
            view[row, MARGIN : MARGIN + across] = value
        swaps.append(exchange_columns(t, view, MARGIN))


    def product(left, weight):
        return jnp.dot(
            left.reshape(-1, left.shape[-1]), weight, preferred_element_type=jnp.float32
        )

    margin = DILATIONS[0]
    block = pl.ds(pl.multiple_of(margin + c * across, 16), across)
    f1[:, block] = hidden.reshape(height, across, state)
    swap = pltpu.make_async_remote_copy(
        src_ref=f1.at[:, block], dst_ref=f1.at[:, block], send_sem=col_s.at[steps - 1],
        recv_sem=col_r.at[steps - 1], device_id=(x, r, twin), device_id_type=MESH_ID,
    )
    swap.start()
    departures.append(swap)

    @pl.when(even_core)
    def _():
        take(context_plan, PAUSE, 1e9)

    pl.when(odd_core)(lambda: twin_waits(contexts[0]))
    swap.wait_recv()

    def convolve(buffer, margin, weight, offset):
        total = None
        for b in range(3):
            more = product(buffer[:, b * margin : b * margin + 2 * across], weight(b))
            total = more if total is None else total + more
        return jnp.maximum(total + offset, 0.0).astype(jnp.bfloat16)

    first = convolve(
        f1, margin, lambda b: jnp.concatenate([w1[s, b] for s in range(n)], axis=0), first_bias
    )
    margin = DILATIONS[1]
    f2[:, margin : margin + 2 * across] = first.reshape(height, 2 * across, -1)
    rims_leave()

    @pl.when(odd_core)
    def _():
        for kind in cells:
            sent_waits(kind)
        twin_waits(contexts[1])

    second = convolve(
        f2, margin, lambda b: jnp.concatenate([w23[0, s, b] for s in range(n)], axis=0),
        second_bias,
    )
    second = second.reshape(height, 2, across, -1)
    for col in range(2):
        f3[col] = second[:, col]

    pl.when(odd_core)(lambda: twin_waits(contexts[2]))

    def last(b):
        return jnp.concatenate([w23[1, s, b] for s in range(n)], axis=0)

    feature = f3[c].reshape(height * across, -1)
    total = product(feature, last(1)) + product(f3[twin], last(2 - 2 * c))
    result = jnp.maximum(total + third_bias, 0.0)
    context = (feature.astype(jnp.float32) + result).astype(jnp.bfloat16)
    out[0] = context.reshape(out.shape[1:])

    @pl.when(even_core)
    def _():
        for kind in contexts:
            sent_waits(kind)

    for copy in departures:
        copy.wait_send()


def grid_device(n, *args):
    frames, cell_w, cell_b, first_w, first_b, second_w, second_b, third_w, third_b = args
    micro, steps, height, across, channels = frames.shape
    state, width = cell_b.shape[0] // 4, first_b.shape[0]
    depth = cell_w.shape[1]
    kinds = max(2 * (depth // 16 if depth % 16 == 0 else 1), 3)
    dma, bf16 = pltpu.SemaphoreType.DMA, jnp.bfloat16
    anywhere, vmem = pl.BlockSpec(memory_space=pl.ANY), pl.BlockSpec(memory_space=pltpu.VMEM)
    return pl.pallas_call(
        functools.partial(grid_kernel, n=n),
        out_shape=pltpu.VMEM((1, height, across, width), bf16),
        in_specs=[anywhere] * 9,
        out_specs=vmem,
        scratch_shapes=[
            pltpu.VMEM((2, n, 9, cell_w.shape[1], 2 * state), bf16),
            pltpu.VMEM((n, 3) + first_w.shape[1:], bf16),
            pltpu.VMEM((2, n, 3) + second_w.shape[1:], bf16),
            pltpu.VMEM((steps, height + 2 * steps, across + 2 * MARGIN, channels), bf16),
            pltpu.VMEM((steps - 1, height + 2 * (steps - 1), across + 2 * MARGIN, state), bf16),
            pltpu.VMEM((height, 2 * (across + DILATIONS[0]), state), bf16),
            pltpu.VMEM((height, 2 * (across + DILATIONS[1]), width), bf16),
            pltpu.VMEM((2, height, across, width), bf16),
            pltpu.VMEM((sum(v.shape[0] for v in (cell_b, first_b, second_b, third_b)),), jnp.float32),
            dma((5,)),
            dma((kinds, n // 2)),
            dma((kinds, n // 2)),
            dma((kinds,)),
            dma((kinds,)),
            dma((3, kinds)),
            dma((kinds,)),
            dma((kinds,)),
            dma((3,)),
            dma((3,)),
            dma((steps,)),
            dma((steps,)),
        ],
        compiler_params=pltpu.CompilerParams(collective_id=1, has_side_effects=True),
    )(*args)


def fits_grid(mesh, frames):
    n, cols = mesh.shape["rows"], mesh.shape["cols"]
    micro, steps, height, across, channels = frames.shape
    return (
        mesh.shape["segment"] == 2 and cols == 2 and n % 2 == 0 and n > 2
        and min(DILATIONS) // height >= n and DILATIONS[-1] == across
        and max(DILATIONS[:-1]) <= across and steps <= height
    )


def solution(mesh):
    kernels = P(None, "rows", None)
    placed = (
        P(None, None, "rows", "cols", None),
        kernels, P(), kernels, P(), kernels, P(), kernels, P(),
    )
    n, cols = mesh.shape["rows"], mesh.shape["cols"]

    def on_device(*args):
        if fits_grid(mesh, args[0]):
            return grid_device(n, *args)
        return per_device(n, cols, mesh.shape["segment"] == 2, *args)

    return jax.shard_map(
        on_device,
        mesh=mesh,
        in_specs=placed,
        out_specs=P("segment", "rows", "cols", None),
        check_vma=False,
    )
```

```python
import functools

import jax
import jax.numpy as jnp
from jax import lax
from jax.experimental import pallas as pl
from jax.experimental.pallas import tpu as pltpu
from jax.sharding import PartitionSpec as P

DILATIONS = (16, 32, 64)
MESH_ID = pl.DeviceIdType.MESH
MARGIN = 16
CELL = (3.2, 1.3, 1.0, 2.6)
SENDS = (0.2, 0.3, 0.4)
CONTEXTS = ((4.0, 1.0, 4.2), (7.0, 1.0, 3.2), (9.0, 1.0, 3.2))
PAUSE = 17.0
DIRECT = (99, 2)


def encoder_kernel(
    frames, cell_w, cell_b, first_w, first_b, second_w, second_b, third_w, third_b,
    out, wc, w1, w2, w3, fp, hp, f1, f2, f3,
    local_sem, ring_s, ring_r, across_s, across_r, pair_s, pair_r, ex_s, ex_r, *, n, cols, shared, row_pads,
):
    seg, r, c = lax.axis_index("segment"), lax.axis_index("rows"), lax.axis_index("cols")
    steps, height, across, channels = frames.shape[1:]
    state = cell_b.shape[-1] // 4
    half = n // 2
    odd = lax.rem(c, 2)
    even_core, odd_core = odd == 0, odd == 1
    sign = 1 - 2 * odd
    parity, pair = lax.rem(r, 2), lax.div(r, 2)
    place = pair + parity * (n - 1 - 2 * pair)

    def rows_at(position):
        upper = lax.div(position, half)
        return 2 * position + upper * (2 * n - 1 - 4 * position)

    behind_rows = [r] + [rows_at(lax.rem(place - sign * k + n, n)) for k in range(1, half + 1)]
    ahead_rows = [r] + [rows_at(lax.rem(place + sign * k + n, n)) for k in range(1, half + 1)]
    following, preceding = ahead_rows[1], behind_rows[1]
    partner = c + 1 - 2 * odd
    ahead_id, partner_id = (seg, following, c), (seg, r, partner)

    reaches = sorted({1} | {s // height for s, pad in zip(DILATIONS, row_pads) if pad})
    offsets = [(0, -1), (0, 1)] + [
        (d * reach, dc) for reach in reaches for d in (-1, 1) for dc in (-1, 0, 1)
    ]

    def present(dr, dc):
        row, col = r + dr, c + dc
        return jnp.logical_and(
            jnp.logical_and(row >= 0, row < n), jnp.logical_and(col >= 0, col < cols)
        )

    inside = {offset: present(*offset) for offset in offsets}

    locals_ = []
    for t in range(steps):
        locals_.append(
            pltpu.make_async_copy(
                frames.at[seg, t],
                fp.at[t, pl.ds(1, height), pl.ds(MARGIN, across)],
                local_sem.at[t],
            )
        )
    stored = (cell_w, first_w, second_w, third_w)
    gathered = (wc, w1, w2, w3)
    own = []
    for ref, whole in zip(stored, gathered):
        taps = whole.shape[1]
        own.append(ref.at[pl.ds((9 - taps) // 2, taps)])
    for a in range(4):
        locals_.append(
            pltpu.make_async_copy(own[a], gathered[a].at[r], local_sem.at[steps + a])
        )
    for t in range(steps):
        fp[t] = jnp.zeros(fp.shape[1:], fp.dtype)
    for t in range(hp.shape[0]):
        hp[t] = jnp.zeros(hp.shape[1:], hp.dtype)
    for buffer in (f1, f2, f3):
        buffer[...] = jnp.zeros(buffer.shape, buffer.dtype)
    for copy in locals_:
        copy.start()

    barrier = pltpu.get_barrier_semaphore()
    expected = jnp.int32(2)
    for target in (following, preceding):
        pl.semaphore_signal(barrier, inc=1, device_id=(seg, target, c), device_id_type=MESH_ID)
    for dr, dc in offsets:
        there = inside[dr, dc]
        expected = expected + there.astype(jnp.int32)

        @pl.when(there)
        def _():
            pl.semaphore_signal(
                barrier, inc=1, device_id=(seg, r + dr, c + dc), device_id_type=MESH_ID
            )

    if shared:
        expected = expected + 1
        pl.semaphore_signal(barrier, inc=1, device_id=(1 - seg, r, c), device_id_type=MESH_ID)
    pl.semaphore_wait(barrier, expected)

    def exchange(number, source_of, buffer, pad, reach, width):
        arrivals, departures = [], []
        for i, (dr, dc) in enumerate((a, b) for a in (-1, 0, 1) for b in (-1, 0, 1)):
            if (dr, dc) == (0, 0) or (dr and not pad):
                continue
            first, span, landing = {
                -1: (0, pad, pad + height), 0: (0, height, pad), 1: (height - pad, pad, 0)
            }[dr]
            left, extent, side = {
                -1: (0, width[1], width[0] + across),
                0: (0, across, width[0]),
                1: (across - width[1], width[1], width[0] - width[1]),
            }[dc]
            copy = pltpu.make_async_remote_copy(
                src_ref=source_of(first, span, left, extent),
                dst_ref=buffer.at[pl.ds(landing, span), pl.ds(side, extent)],
                send_sem=ex_s.at[number, i],
                recv_sem=ex_r.at[number, i],
                device_id=(seg, r + dr * reach, c + dc),
                device_id_type=MESH_ID,
            )
            there, behind = inside[dr * reach, dc], inside[-dr * reach, -dc]
            pl.when(there)(copy.start)
            departures.append((there, copy))
            arrivals.append((behind, copy))

        def arrive():
            for behind, copy in arrivals:
                pl.when(behind)(copy.wait_recv)

        def depart():
            for there, copy in departures:
                pl.when(there)(copy.wait_send)

        return arrive, depart

    def block_of(buffer, pad, margin):
        return lambda first, span, left, extent: buffer.at[
            pl.ds(pad + first, span), pl.ds(margin + left, extent)
        ]

    departs = []
    frame_arrivals = []
    for t in range(steps):
        arrive, depart = exchange(
            t,
            lambda first, span, left, extent, t=t: frames.at[
                seg, t, pl.ds(first, span), pl.ds(left, extent)
            ],
            fp.at[t], 1, 1, (MARGIN, MARGIN),
        )
        frame_arrivals.append(arrive)
        departs.append(depart)

    parts = (2 * seg, 1, 2 * (1 - seg)) if shared else (0, 1, 2)
    carried = range(2) if shared else range(3)

    def slot(a, part, k):
        span = gathered[a].shape[1] // 3
        source = behind_rows[k] if k >= 0 else ahead_rows[-k]
        return gathered[a].at[source, pl.ds(parts[part] * span, span)]

    def ring_copy(a, part, k, sent=True):
        span = gathered[a].shape[1] // 3
        place_of = slot(a, part, k if sent else k + 1)
        start = (9 - 3 * span) // 2 + parts[part] * span
        return pltpu.make_async_remote_copy(
            src_ref=stored[a].at[pl.ds(start, span)] if sent and k == 0 else place_of,
            dst_ref=place_of,
            send_sem=ring_s.at[a, part, k],
            recv_sem=ring_r.at[a, part, k],
            device_id=ahead_id,
            device_id_type=MESH_ID,
        )

    def across_copy(a, k, sent=True):
        piece = slot(a, 0 if sent else 2, k)
        return pltpu.make_async_remote_copy(
            src_ref=piece, dst_ref=piece, send_sem=across_s.at[a, k], recv_sem=across_r.at[a, k],
            device_id=(1 - seg, r, c), device_id_type=MESH_ID,
        )

    def pair_copy(a, part, k, direction):
        piece = slot(a, part, direction * k)
        return pltpu.make_async_remote_copy(
            src_ref=piece, dst_ref=piece, send_sem=pair_s.at[a, part, k],
            recv_sem=pair_r.at[a, part, k], device_id=partner_id, device_id_type=MESH_ID,
        )

    def longer(a):
        return even_core if a == 0 else odd_core

    def guarded(condition, act):
        if condition is None:
            act()
        else:
            pl.when(condition)(act)

    def ring_send(a, part, k):
        guarded(longer(a) if k == half - 1 else None, ring_copy(a, part, k).start)

    def own_send(a):
        for part in carried:
            ring_send(a, part, 0)

    def ring_step(a, k):
        def act():
            for part in carried:
                ring_copy(a, part, k - 1, False).wait_recv()
                if k < half:
                    ring_send(a, part, k)
                if shared and part == 0:
                    across_copy(a, k).start()
                pair_copy(a, part, k, 1).start()

        guarded(longer(a) if k == half else None, act)

    def across_step(a, k):
        def act():
            across_copy(a, k, False).wait_recv()
            pair_copy(a, 2, k, 1).start()

        if shared:
            guarded(longer(a) if k == half else None, act)

    def pair_waits(a):
        shorter = odd_core if a == 0 else even_core
        for k in range(1, half + 1):
            for part in range(3):
                guarded(
                    shorter if k == half else None, pair_copy(a, part, k, -1).wait_recv
                )

    context_steps = list(range(1, half + 1))
    quarter = max(1, half // 4)

    def context_ring(count):
        for _ in range(min(count, len(context_steps))):
            k = context_steps.pop(0)
            for a in (1, 2, 3):
                ring_step(a, k)
            if k > 1:
                for a in (1, 2, 3):
                    across_step(a, k - 1)

    own_send(0)
    for k in range(1, half + 1):
        ring_step(0, k)
        if k > 1:
            across_step(0, k - 1)
        if k == 1:
            for a in (1, 2, 3):
                own_send(a)
        else:
            context_ring(1)
    context_ring(quarter)
    across_step(0, half)

    for copy in locals_:
        copy.wait()
    for arrive in frame_arrivals:
        arrive()
    pair_waits(0)

    bias = cell_b[...].reshape(1, -1)
    per = wc.shape[2]
    frame_sources = channels // per

    def tap_columns(buffer):
        taps = []
        for row in range(height + 2):
            wide = buffer[row].astype(jnp.float32)
            length = wide.shape[0]
            taps.append(
                [
                    pltpu.roll(wide, 1, 0)[MARGIN : MARGIN + across].astype(jnp.bfloat16),
                    buffer[row, MARGIN : MARGIN + across],
                    pltpu.roll(wide, length - 1, 0)[MARGIN : MARGIN + across].astype(
                        jnp.bfloat16
                    ),
                ]
            )
        return taps

    def gate_part(buffer, sources):
        taps = tap_columns(buffer)
        left = jnp.concatenate(
            [
                jnp.concatenate([taps[row + a][b] for row in range(height)], axis=0)
                for a in range(3)
                for b in range(3)
            ],
            axis=1,
        )
        right = jnp.concatenate([wc[s, t] for t in range(9) for s in sources], axis=0)
        return jnp.dot(left, right, preferred_element_type=jnp.float32)

    def update(gates, memory):
        inflow = jax.nn.sigmoid(gates[:, :state])
        forget = jax.nn.sigmoid(gates[:, state : 2 * state])
        output = jax.nn.sigmoid(gates[:, 2 * state : 3 * state])
        fresh = inflow * jnp.tanh(gates[:, 3 * state :])
        memory = fresh if memory is None else forget * memory + fresh
        return (output * jnp.tanh(memory)).astype(jnp.bfloat16), memory

    seen, unseen = range(frame_sources), range(frame_sources, n)
    hidden, memory = update(gate_part(fp.at[0], seen) + bias, None)
    for t in range(1, steps):
        view = hp.at[t - 1]
        for row in range(height):
            view[1 + row, MARGIN : MARGIN + across] = hidden[row * across : (row + 1) * across]
        arrive, depart = exchange(
            steps + t - 1, block_of(view, 1, MARGIN), view, 1, 1, (MARGIN, MARGIN)
        )
        departs.append(depart)
        context_ring(quarter)
        gates = gate_part(fp.at[t], seen) + bias
        context_ring(quarter)
        arrive()
        hidden, memory = update(gates + gate_part(view, unseen), memory)

    feature = hidden
    layers = ((f1, w1, first_b), (f2, w2, second_b), (f3, w3, third_b))
    for i, (buffer, weight, offset) in enumerate(layers):
        spacing, pad = DILATIONS[i], row_pads[i]
        for row in range(height):
            buffer[pad + row, spacing : spacing + across] = feature[
                row * across : (row + 1) * across
            ]
        arrive, depart = exchange(
            2 * steps - 1 + i, block_of(buffer, pad, spacing), buffer, pad,
            spacing // height, (spacing, spacing),
        )
        departs.append(depart)
        if i == 0:
            context_ring(len(context_steps))
            for a in (1, 2, 3):
                across_step(a, half)
        pair_waits(i + 1)
        arrive()
        total = None
        taps = weight.shape[1]
        for t in range(taps):
            a, b = t // 3, t % 3
            left = buffer[a * pad : a * pad + height, b * spacing : b * spacing + across]
            left = left.reshape(height * across, left.shape[-1])
            right = jnp.concatenate([weight[s, t] for s in range(n)], axis=0)
            product = jnp.dot(left, right, preferred_element_type=jnp.float32)
            total = product if total is None else total + product
        result = jnp.maximum(total + offset[...].reshape(1, -1), 0.0)
        if i < 2:
            feature = result.astype(jnp.bfloat16)
    context = (feature.astype(jnp.float32) + result).astype(jnp.bfloat16)
    out[0] = context.reshape(out.shape[1:])

    for depart in departs:
        depart()
    for a in range(4):
        for k in range(half):
            for part in carried:
                guarded(
                    longer(a) if k == half - 1 else None, ring_copy(a, part, k).wait_send
                )
        for k in range(1, half + 1):
            for part in range(3):
                guarded(longer(a) if k == half else None, pair_copy(a, part, k, 1).wait_send)
            if shared:
                guarded(longer(a) if k == half else None, across_copy(a, k).wait_send)


def per_device(n, cols, shared, *args):
    frames, cell_w, cell_b, first_w, first_b, second_w, second_b, third_w, third_b = args
    micro, steps, height, across, channels = frames.shape
    state, width = cell_b.shape[0] // 4, first_b.shape[0]
    row_pads = tuple(height if s // height < n else 0 for s in DILATIONS)

    def slots(weight, pad):
        return pltpu.VMEM((n, 9 if pad else 3) + weight.shape[1:], weight.dtype)

    def field(spacing, pad, depth):
        return pltpu.VMEM((height + 2 * pad, across + 2 * spacing, depth), jnp.bfloat16)

    half = n // 2
    exchanges = 2 * steps - 1 + 3
    dma = pltpu.SemaphoreType.DMA
    anywhere, vmem = pl.BlockSpec(memory_space=pl.ANY), pl.BlockSpec(memory_space=pltpu.VMEM)
    return pl.pallas_call(
        functools.partial(encoder_kernel, n=n, cols=cols, shared=shared, row_pads=row_pads),
        out_shape=jax.ShapeDtypeStruct((1, height, across, width), jnp.bfloat16),
        in_specs=[anywhere, anywhere, vmem, anywhere, vmem, anywhere, vmem, anywhere, vmem],
        out_specs=vmem,
        scratch_shapes=[
            slots(cell_w, 1),
            slots(first_w, row_pads[0]),
            slots(second_w, row_pads[1]),
            slots(third_w, row_pads[2]),
            pltpu.VMEM((steps, height + 2, across + 2 * MARGIN, channels), jnp.bfloat16),
            pltpu.VMEM((steps - 1, height + 2, across + 2 * MARGIN, state), jnp.bfloat16),
            field(DILATIONS[0], row_pads[0], state),
            field(DILATIONS[1], row_pads[1], width),
            field(DILATIONS[2], row_pads[2], width),
            dma((steps + 4,)),
            dma((4, 3, half)),
            dma((4, 3, half)),
            dma((4, half + 1)),
            dma((4, half + 1)),
            dma((4, 3, half + 1)),
            dma((4, 3, half + 1)),
            dma((exchanges, 9)),
            dma((exchanges, 9)),
        ],
        compiler_params=pltpu.CompilerParams(collective_id=0, has_side_effects=True),
    )(
        frames, cell_w, cell_b, first_w, first_b, second_w, second_b,
        third_w, third_b,
    )


def grid_kernel(
    frames, cell_w, cell_b, first_w, first_b, second_w, second_b, third_w, third_b,
    out, wc, w1, w23, fp, hp, f1, f2, f3, biases,
    local_sem, z_sem, y_sem, x_sem, relay_sem, link_sem, twin_s, twin_r, ex_s, ex_r, col_s, col_r,
    *, n,
):
    x, r, c = lax.axis_index("segment"), lax.axis_index("rows"), lax.axis_index("cols")
    steps, height, across, channels = frames.shape[1:]
    state = cell_b.shape[-1] // 4
    planes = n // 2
    reach = planes - 1
    z, y = lax.div(r, 2), lax.rem(r, 2)
    ry = r + 1 - 2 * y
    twin = 1 - c
    even_core, odd_core = c == 0, c == 1

    def run(condition, act):
        if condition is None:
            act()
        else:
            pl.when(condition)(act)

    near_side = jnp.where(z < planes - 1 - z, z, planes - 1 - z)
    long_side = jnp.where(z < planes - 1 - z, 1, -1)

    def other(j):
        paired = j < 2 * near_side
        k = jnp.where(paired, j // 2 + 1, j + 1 - near_side)
        return z + jnp.where(paired, long_side * (1 - 2 * (j % 2)), long_side) * k

    others = [other(j) for j in range(reach)]

    pads = [steps - t for t in range(steps)]
    locals_ = [
        pltpu.make_async_copy(
            cell_w.at[:, :, pl.ds(half * 2 * state, 2 * state)], wc.at[half, r],
            local_sem.at[0],
        )
        for half in range(2)
    ]
    locals_.append(pltpu.make_async_copy(first_w.at[pl.ds(3, 3)], w1.at[r], local_sem.at[1]))
    for half, weight in enumerate((second_w, third_w)):
        locals_.append(
            pltpu.make_async_copy(weight.at[pl.ds(3, 3)], w23.at[half, r], local_sem.at[2])
        )
    for t in range(steps):
        locals_.append(
            pltpu.make_async_copy(
                frames.at[x, t],
                fp.at[t, pl.ds(pads[t], height), pl.ds(MARGIN, across)],
                local_sem.at[3],
            )
        )
    offset = 0
    spans = []
    for vector in (cell_b, first_b, second_b, third_b):
        length = vector.shape[0]
        spans.append((offset, length))
        locals_.append(
            pltpu.make_async_copy(vector, biases.at[pl.ds(offset, length)], local_sem.at[4])
        )
        offset += length
    for copy in locals_:
        copy.start()

    def local_wait(number, ref):
        pltpu.make_async_copy(ref, ref, local_sem.at[number]).wait()

    def row_inside(row):
        return jnp.logical_and(row >= 0, row < n)

    barrier = pltpu.get_barrier_semaphore()
    expected = jnp.int32(2 + reach)
    pl.semaphore_signal(barrier, inc=1, device_id=(1 - x, r, c), device_id_type=MESH_ID)
    pl.semaphore_signal(barrier, inc=1, device_id=(x, r, twin), device_id_type=MESH_ID)
    for plane in others:
        pl.semaphore_signal(
            barrier, inc=1, device_id=(x, 2 * plane + y, c), device_id_type=MESH_ID
        )
    for d in (-1, 1):
        there = row_inside(r + d)
        expected = expected + 2 * there.astype(jnp.int32)

        @pl.when(there)
        def _(d=d):
            for core in (c, twin):
                pl.semaphore_signal(
                    barrier, inc=1, device_id=(x, r + d, core), device_id_type=MESH_ID
                )

    pl.semaphore_wait(barrier, expected)

    depth = wc.shape[3]
    part_rows = 16 if depth % 16 == 0 else depth
    parts = [
        (half, pl.ds(first, part_rows)) for half in range(2) for first in range(0, depth, part_rows)
    ]
    cells = [("cell", a) for a in range(len(parts))]
    contexts = [("context", a) for a in range(3)]

    def taps_of(kind):
        return wc.shape[2] if kind[0] == "cell" else w1.shape[1]

    def complete(kind):
        return kind == ("context", 0)

    def carried(kind):
        if complete(kind):
            return everything(kind)
        larger = (taps_of(kind) + 1) // 2
        return (taps_of(kind) - larger) * x, larger

    def only_here(kind, there=False):
        larger = (taps_of(kind) + 1) // 2
        return larger * (1 - x if there else x), taps_of(kind) - larger

    def everything(kind):
        return 0, taps_of(kind)

    def shards(kind, s, taps):
        taps = pl.ds(*taps)
        if kind[0] == "cell":
            half, rows = parts[kind[1]]
            return wc.at[half, s, taps, rows]
        if kind[1] == 0:
            return w1.at[s, taps]
        return w23.at[kind[1] - 1, s, taps]

    def several(kind, count, taps):
        return shards(kind, pl.ds(0, count), taps)

    def stored(kind, taps):
        if kind[0] == "cell":
            half, rows = parts[kind[1]]
            return cell_w.at[pl.ds(*taps), rows, pl.ds(half * 2 * state, 2 * state)]
        whole = (first_w, second_w, third_w)[kind[1]]
        return whole.at[pl.ds((whole.shape[0] - taps_of(kind)) // 2 + taps[0], taps[1])]

    twin_id, beside, opposite = (x, r, twin), (x, ry, c), (1 - x, r, c)
    departures = []

    def remote(source, ref, sent, landed, device):
        return pltpu.make_async_remote_copy(
            src_ref=source, dst_ref=ref, send_sem=sent, recv_sem=landed,
            device_id=device, device_id_type=MESH_ID,
        )

    def send(kind, s, taps, way, landed, device, own=False):
        ref = shards(kind, s, taps)
        source = stored(kind, taps) if own else ref
        remote(source, ref, link_sem.at[way, kind[1]], landed, device).start()

    def hand_over(kind, s, taps):
        ref = shards(kind, s, taps)
        remote(ref, ref, twin_s.at[kind[1]], twin_r.at[kind[1]], twin_id).start()

    def receive(kind, ref, landed):
        remote(ref, ref, link_sem.at[0, kind[1]], landed, twin_id).wait_recv()

    def far(kind):
        return DIRECT[kind[0] == "context"]

    def distance(j):
        return jnp.abs(others[j] - z)

    def z_send(kind, j):
        def act():
            device = (x, 2 * others[j] + y, c)
            send(kind, r, carried(kind), 0, z_sem.at[kind[1], z], device, own=True)

        if j < far(kind):
            act()
        else:
            pl.when(distance(j) <= far(kind))(act)

    def z_forward(kind, j):
        plane = others[j]
        beyond = z + jnp.where(plane < z, 1, -1)
        there = jnp.logical_and(beyond >= 0, beyond < planes)

        @pl.when(jnp.logical_and(there, distance(j) >= far(kind)))
        def _():
            device = (x, 2 * beyond + y, c)
            send(kind, 2 * plane + y, carried(kind), 0, z_sem.at[kind[1], plane], device)

    def whole_own(kind):
        return True

    def y_taps(kind, j):
        return everything(kind) if whole_own(kind) and j < 0 else carried(kind)

    def relays(kind):
        return range(reach if complete(kind) else 0, reach)

    def own_send(kind, _):
        send(kind, r, y_taps(kind, -1), 1, y_sem.at[kind[1], z], beside, own=True)

    def z_step(kind, j):
        plane = others[j]
        s = 2 * plane + y
        receive(kind, shards(kind, s, carried(kind)), z_sem.at[kind[1], plane])
        if j + 1 >= far(kind) and far(kind) < reach:
            z_forward(kind, j)
        send(kind, s, carried(kind), 1, y_sem.at[kind[1], plane], beside)
        if not complete(kind):
            send(kind, s, only_here(kind), 2, x_sem.at[kind[1]], opposite)
        if complete(kind):
            hand_over(kind, s, carried(kind))

    def y_step(kind, j):
        plane = z if j < 0 else others[j]
        s = 2 * plane + 1 - y
        receive(kind, shards(kind, s, y_taps(kind, j)), y_sem.at[kind[1], plane])
        if j in relays(kind):
            send(kind, s, only_here(kind), 1, relay_sem.at[kind[1]], opposite)
        hand_over(kind, s, y_taps(kind, j))

    def x_step(kind, _):
        taps = only_here(kind, True)
        receive(kind, several(kind, reach, taps), x_sem.at[kind[1]])
        for plane in others:
            hand_over(kind, 2 * plane + y, everything(kind))

    def relay_step(kind, _):
        taps = only_here(kind, True)
        receive(kind, several(kind, len(relays(kind)), taps), relay_sem.at[kind[1]])
        for j in relays(kind):
            plane = z if j < 0 else others[j]
            hand_over(kind, 2 * plane + 1 - y, taps)

    def twin_waits(kind):
        ref = several(kind, n - 1, everything(kind))
        remote(ref, ref, twin_s.at[kind[1]], twin_r.at[kind[1]], twin_id).wait_recv()

    def sent_waits(kind):
        def sent(count, taps, sem):
            ref = several(kind, count, taps)
            remote(ref, ref, sem, twin_r.at[kind[1]], twin_id).wait_send()

        def sent_along_z(place):
            direct = sum(1 for p in range(planes) if 0 < abs(p - place) <= far(kind))
            passed = sum(
                1 for p in range(planes) for step in (-1, 1)
                if (place - p) * step >= far(kind) and 0 <= place + step < planes
            )
            sent(direct + passed, carried(kind), link_sem.at[0, kind[1]])

        if far(kind) >= reach:
            sent(reach, carried(kind), link_sem.at[0, kind[1]])
        else:
            for place in range(planes):
                pl.when(z == place)(functools.partial(sent_along_z, place))
        sent(planes, everything(kind), link_sem.at[1, kind[1]])
        if not complete(kind):
            sent(reach, only_here(kind), link_sem.at[2, kind[1]])
        sent(n - 1, everything(kind), twin_s.at[kind[1]])

    def plan_of(kinds, sends, times):
        plan = [(when, z_send, kind, j) for kind, when in zip(kinds, sends) for j in range(reach)]
        plan += [(when, own_send, kind, 0) for kind, when in zip(kinds, sends)]
        for kind, (start, pace, hop) in zip(kinds, times):
            plan.append((start + 0.5, y_step, kind, -1))
            for j in range(reach):
                there = start + pace * j
                plan.append((there, z_step, kind, j))
                plan.append((there + hop, y_step, kind, j))
            if not complete(kind):
                plan.append((there + hop - 0.1, x_step, kind, 0))
                plan.append((there + 2 * hop, relay_step, kind, 0))
        return sorted(plan, key=lambda entry: entry[0])

    spread = [CELL[0] + CELL[1] * a for a in range(len(cells))]
    cell_plan = plan_of(cells, [0.0] * len(cells), [(at,) + CELL[2:] for at in spread])
    context_plan = plan_of(contexts, SENDS, CONTEXTS)

    def take(plan, first, last):
        for when, step, kind, j in plan:
            if first <= when < last:
                step(kind, j)

    early = 0.1
    pl.when(odd_core)(lambda: take(cell_plan, 0.0, early))

    side = across + MARGIN
    rims = sum(pads)
    for d in (-1, 0, 1):
        there = row_inside(r + d) if d else None

        def rim(act, d=d):
            for t in range(steps):
                pad = pads[t]
                first, span, landing = {
                    -1: (0, pad, pad + height), 0: (0, height, pad), 1: (height - pad, pad, 0)
                }[d]
                for core in (c, twin):
                    if core is c and d == 0:
                        continue
                    if core is c:
                        left, extent, place = 0, across, MARGIN
                    else:
                        left = pl.multiple_of((1 - c) * (across - MARGIN), 16)
                        extent, place = MARGIN, pl.multiple_of(c * (across + MARGIN), 16)
                    act(
                        remote(
                            frames.at[x, t, pl.ds(first, span), pl.ds(left, extent)],
                            fp.at[t, pl.ds(landing, span), pl.ds(place, extent)],
                            ex_s.at[d + 1], ex_r.at[d + 1], (x, r + d, core),
                        )
                    )

        run(there, lambda: rim(lambda copy: copy.start()))

    def rim_ref(d):
        if d == 0:
            return fp.at[:, pl.ds(0, height), pl.ds(0, MARGIN)]
        return fp.at[0, pl.ds(0, rims), pl.ds(0, side)]

    def rims_arrive():
        for d in (-1, 0, 1):
            ref = rim_ref(d)
            copy = remote(ref, ref, ex_s.at[d + 1], ex_r.at[d + 1], twin_id)
            run(row_inside(r - d) if d else None, copy.wait_recv)

    def rims_leave():
        for d in (-1, 0, 1):
            ref = rim_ref(d)
            copy = remote(ref, ref, ex_s.at[d + 1], ex_r.at[d + 1], twin_id)
            run(row_inside(r + d) if d else None, copy.wait_send)

    for t in range(steps):
        pad = pads[t]
        total_rows = height + 2 * pad

        def blank(ref, first, count, left, extent):
            ref[first : first + count, left : left + extent] = jnp.zeros(
                (count, extent, ref.shape[-1]), ref.dtype
            )

        @pl.when(r == 0)
        def _(t=t, pad=pad):
            blank(fp.at[t], 0, pad, 0, across + 2 * MARGIN)

        @pl.when(r == n - 1)
        def _(t=t, pad=pad):
            blank(fp.at[t], pad + height, pad, 0, across + 2 * MARGIN)

        @pl.when(even_core)
        def _(t=t, total_rows=total_rows):
            blank(fp.at[t], 0, total_rows, 0, MARGIN)

        @pl.when(odd_core)
        def _(t=t, total_rows=total_rows):
            blank(fp.at[t], 0, total_rows, MARGIN + across, MARGIN)

    for ref, margin in ((f1, DILATIONS[0]), (f2, DILATIONS[1])):
        blank(ref, 0, ref.shape[0], 0, margin)
        blank(ref, 0, ref.shape[0], margin + 2 * across, margin)
    for ref, margin in [(hp.at[t], MARGIN) for t in range(steps - 1)]:
        @pl.when(even_core)
        def _(ref=ref, margin=margin):
            blank(ref, 0, ref.shape[0], 0, margin)

        @pl.when(odd_core)
        def _(ref=ref, margin=margin):
            blank(ref, 0, ref.shape[0], margin + across, margin)

    pl.when(odd_core)(lambda: take(cell_plan, early, 1e9))

    @pl.when(even_core)
    def _():
        take(context_plan, 0.0, PAUSE)
        for kind in cells:
            twin_waits(kind)

    local_wait(0, wc.at[:, r])
    local_wait(1, w1.at[r])
    local_wait(2, w23.at[:, r])
    local_wait(3, fp.at[:, pl.ds(0, height), pl.ds(0, across)])
    local_wait(4, biases)
    rims_arrive()

    cell_bias, first_bias, second_bias, third_bias = [
        biases[at : at + length].reshape(1, -1) for at, length in spans
    ]
    per = wc.shape[3]
    frame_sources = channels // per

    def tap_columns(buffer, count):
        taps = []
        for row in range(count):
            wide_row = buffer[row].astype(jnp.float32)
            length = wide_row.shape[0]
            taps.append(
                [
                    pltpu.roll(wide_row, 1, 0)[MARGIN : MARGIN + across].astype(jnp.bfloat16),
                    buffer[row, MARGIN : MARGIN + across],
                    pltpu.roll(wide_row, length - 1, 0)[MARGIN : MARGIN + across].astype(
                        jnp.bfloat16
                    ),
                ]
            )
        return taps

    def columns_of(buffer, count):
        taps = tap_columns(buffer, count + 2)
        return jnp.concatenate(
            [
                jnp.concatenate([taps[row + a][b] for row in range(count)], axis=0)
                for a in range(3)
                for b in range(3)
            ],
            axis=1,
        )

    def gate_part(left, sources):
        return [
            jnp.dot(
                left,
                jnp.concatenate([wc[half, s, t] for t in range(9) for s in sources], axis=0),
                preferred_element_type=jnp.float32,
            )
            for half in range(2)
        ]

    def update(gates, memory):
        inflow = jax.nn.sigmoid(gates[0][:, :state])
        output = jax.nn.sigmoid(gates[1][:, :state])
        fresh = inflow * jnp.tanh(gates[1][:, state:])
        if memory is None:
            memory = fresh
        else:
            memory = jax.nn.sigmoid(gates[0][:, state:]) * memory + fresh
        return (output * jnp.tanh(memory)).astype(jnp.bfloat16), memory

    swaps = []

    def exchange_columns(number, buffer, margin):
        sent = pl.multiple_of((1 - c) * across + c * margin, 16)
        landing = pl.multiple_of(c * (margin + across), 16)
        copy = pltpu.make_async_remote_copy(
            src_ref=buffer.at[:, pl.ds(sent, margin)],
            dst_ref=buffer.at[:, pl.ds(landing, margin)],
            send_sem=col_s.at[number],
            recv_sem=col_r.at[number],
            device_id=(x, r, twin),
            device_id_type=MESH_ID,
        )
        copy.start()
        departures.append(copy)
        return copy

    seen, unseen = range(frame_sources), range(frame_sources, n)
    counts = [height + 2 * (steps - 1 - t) for t in range(steps)]
    lefts = jnp.concatenate(
        [columns_of(fp.at[t], counts[t]) for t in range(steps)], axis=0
    )
    frame_gates = gate_part(lefts, seen)
    start = 0
    memory = None
    for t in range(steps):
        length = counts[t] * across
        gates = [
            part[start : start + length] + cell_bias[:, half * 2 * state : (half + 1) * 2 * state]
            for half, part in enumerate(frame_gates)
        ]
        start += length
        if t:
            swaps[-1].wait_recv()
            extra = gate_part(columns_of(hp.at[t - 1], counts[t]), unseen)
            gates = [one + more for one, more in zip(gates, extra)]
            memory = memory[across : memory.shape[0] - across]
        hidden, memory = update(gates, memory)
        if t == steps - 1:
            break
        view = hp.at[t]
        outside = steps - 1 - t
        for row in range(counts[t]):
            value = hidden[row * across : (row + 1) * across]
            if row < outside or row >= counts[t] - outside:
                place = r * height + row - outside
                valid = jnp.logical_and(place >= 0, place < n * height)
                value = jnp.where(valid, value, jnp.zeros_like(value))
            view[row, MARGIN : MARGIN + across] = value
        swaps.append(exchange_columns(t, view, MARGIN))


    def product(left, weight):
        return jnp.dot(
            left.reshape(-1, left.shape[-1]), weight, preferred_element_type=jnp.float32
        )

    margin = DILATIONS[0]
    block = pl.ds(pl.multiple_of(margin + c * across, 16), across)
    f1[:, block] = hidden.reshape(height, across, state)
    swap = pltpu.make_async_remote_copy(
        src_ref=f1.at[:, block], dst_ref=f1.at[:, block], send_sem=col_s.at[steps - 1],
        recv_sem=col_r.at[steps - 1], device_id=(x, r, twin), device_id_type=MESH_ID,
    )
    swap.start()
    departures.append(swap)

    @pl.when(even_core)
    def _():
        take(context_plan, PAUSE, 1e9)

    pl.when(odd_core)(lambda: twin_waits(contexts[0]))
    swap.wait_recv()

    def convolve(buffer, margin, weight, offset):
        total = None
        for b in range(3):
            more = product(buffer[:, b * margin : b * margin + 2 * across], weight(b))
            total = more if total is None else total + more
        return jnp.maximum(total + offset, 0.0).astype(jnp.bfloat16)

    first = convolve(
        f1, margin, lambda b: jnp.concatenate([w1[s, b] for s in range(n)], axis=0), first_bias
    )
    margin = DILATIONS[1]
    f2[:, margin : margin + 2 * across] = first.reshape(height, 2 * across, -1)
    rims_leave()

    @pl.when(odd_core)
    def _():
        for kind in cells:
            sent_waits(kind)
        twin_waits(contexts[1])

    second = convolve(
        f2, margin, lambda b: jnp.concatenate([w23[0, s, b] for s in range(n)], axis=0),
        second_bias,
    )
    second = second.reshape(height, 2, across, -1)
    for col in range(2):
        f3[col] = second[:, col]

    pl.when(odd_core)(lambda: twin_waits(contexts[2]))

    def last(b):
        return jnp.concatenate([w23[1, s, b] for s in range(n)], axis=0)

    feature = f3[c].reshape(height * across, -1)
    total = product(feature, last(1)) + product(f3[twin], last(2 - 2 * c))
    result = jnp.maximum(total + third_bias, 0.0)
    context = (feature.astype(jnp.float32) + result).astype(jnp.bfloat16)
    out[0] = context.reshape(out.shape[1:])

    @pl.when(even_core)
    def _():
        for kind in contexts:
            sent_waits(kind)

    for copy in departures:
        copy.wait_send()


def grid_device(n, *args):
    frames, cell_w, cell_b, first_w, first_b, second_w, second_b, third_w, third_b = args
    micro, steps, height, across, channels = frames.shape
    state, width = cell_b.shape[0] // 4, first_b.shape[0]
    depth = cell_w.shape[1]
    kinds = max(2 * (depth // 16 if depth % 16 == 0 else 1), 3)
    dma, bf16 = pltpu.SemaphoreType.DMA, jnp.bfloat16
    anywhere, vmem = pl.BlockSpec(memory_space=pl.ANY), pl.BlockSpec(memory_space=pltpu.VMEM)
    return pl.pallas_call(
        functools.partial(grid_kernel, n=n),
        out_shape=pltpu.VMEM((1, height, across, width), bf16),
        in_specs=[anywhere] * 9,
        out_specs=vmem,
        scratch_shapes=[
            pltpu.VMEM((2, n, 9, cell_w.shape[1], 2 * state), bf16),
            pltpu.VMEM((n, 3) + first_w.shape[1:], bf16),
            pltpu.VMEM((2, n, 3) + second_w.shape[1:], bf16),
            pltpu.VMEM((steps, height + 2 * steps, across + 2 * MARGIN, channels), bf16),
            pltpu.VMEM((steps - 1, height + 2 * (steps - 1), across + 2 * MARGIN, state), bf16),
            pltpu.VMEM((height, 2 * (across + DILATIONS[0]), state), bf16),
            pltpu.VMEM((height, 2 * (across + DILATIONS[1]), width), bf16),
            pltpu.VMEM((2, height, across, width), bf16),
            pltpu.VMEM((sum(v.shape[0] for v in (cell_b, first_b, second_b, third_b)),), jnp.float32),
            dma((5,)),
            dma((kinds, n // 2)),
            dma((kinds, n // 2)),
            dma((kinds,)),
            dma((kinds,)),
            dma((3, kinds)),
            dma((kinds,)),
            dma((kinds,)),
            dma((3,)),
            dma((3,)),
            dma((steps,)),
            dma((steps,)),
        ],
        compiler_params=pltpu.CompilerParams(collective_id=1, has_side_effects=True),
    )(*args)


def fits_grid(mesh, frames):
    n, cols = mesh.shape["rows"], mesh.shape["cols"]
    micro, steps, height, across, channels = frames.shape
    return (
        mesh.shape["segment"] == 2 and cols == 2 and n % 2 == 0 and n > 2
        and min(DILATIONS) // height >= n and DILATIONS[-1] == across
        and max(DILATIONS[:-1]) <= across and steps <= height
    )


def solution(mesh):
    kernels = P(None, "rows", None)
    placed = (
        P(None, None, "rows", "cols", None),
        kernels, P(), kernels, P(), kernels, P(), kernels, P(),
    )
    n, cols = mesh.shape["rows"], mesh.shape["cols"]

    def on_device(*args):
        if fits_grid(mesh, args[0]):
            return grid_device(n, *args)
        return per_device(n, cols, mesh.shape["segment"] == 2, *args)

    return jax.shard_map(
        on_device,
        mesh=mesh,
        in_specs=placed,
        out_specs=P("segment", "rows", "cols", None),
        check_vma=False,
    )
```
